32 devices in a mesh: mode: 4 (over y, x), tm: 8 (over z, core).
Axes of the slice: x: 2, y: 2, z: 4, core: 2. Of those that a mesh axis runs over, the one named last changes fastest.
Arguments:
- field: float32 [96, 2, 4096], P('mode', None, 'tm'), may hold values from -6 to 6
- modes: float32 [96, 1024], P(None, 'mode'), may hold values from -0.1875 to 0.1875
- betas: float32 [96, 4], P('mode'), may hold values from -4 to 4
Outputs:
- field_out: float32 [96, 2, 4096], P('mode', None, 'tm')
The draws below stay inside these ranges and needn't reach their ends.
All inputs are finite; a program needn't handle non-finite values.
Results may differ from the reference program's by a relative error of at most 0.0003.
Values sent between devices are 32-bit elements; how exact they have to be, the bound alone decides.
No kernel may reach another device: no remote copies, remote signals or barrier semaphores. Data moves between devices by JAX's collectives and lax.ppermute only.
A program may use at most 64 MiB of HBM per device.

```python
import jax
import jax.numpy as jnp
from jax import lax

MODES = 96
GRID = 1024
RAMAN_TAPS = 256
ITERS = 2
TIME = 4096
N_MODE = 4


def block_scale(own_key, shape, split, low, largest):
    factor_of = 1.0
    for axis_at, shards_of in split:
        steps = jax.random.uniform(jax.random.fold_in(jax.random.fold_in(own_key, 6), axis_at), (shards_of,), jnp.float32, low / len(split), largest / len(split))
        factor_of = factor_of * jnp.repeat(jnp.exp(steps), shape[axis_at] // shards_of).reshape((-1,) + (1,) * (len(shape) - 1 - axis_at))
    return factor_of


def normal_values(rng, extent, deviation, limit, cuts=(), kind=jnp.bfloat16):
    values = deviation * jax.random.normal(rng, extent, jnp.float32)
    if cuts:
        values = values * block_scale(rng, extent, cuts, -0.22, 0.18)
    return jnp.clip(values, -limit, limit).astype(kind)


def setup_inputs(seed: int = 0) -> dict:
    key_of = jax.random.split(jax.random.key(seed), 4)
    return {
        "field": normal_values(key_of[0], (MODES, 2, TIME), 1.0, 6.0, ((0, 4), (2, 8)), jnp.float32),
        "modes": normal_values(key_of[1], (MODES, GRID), GRID ** -0.5, 0.1875, ((1, 4),), jnp.float32),
        "betas": jnp.clip(jax.random.uniform(key_of[2], (MODES, 4), jnp.float32, -4.0, 4.0) * block_scale(key_of[2], (MODES, 4), ((0, 4),), -0.4, 0.0), -4.0, 4.0),
    }


RAMAN_SHARE = 0.18
KERR_GAIN = 6.0


def kernel_raw(positions):
    spacing = 256.0 / RAMAN_TAPS
    return jnp.exp(-positions * spacing / 32.0) * jnp.sin(positions * spacing / 12.2)


def reference(field, modes, betas):
    positions = jnp.arange(1, RAMAN_TAPS + 1).astype(jnp.float32)
    raw_taps = kernel_raw(positions)
    kernel = raw_taps / jnp.sum(raw_taps)
    padded = jnp.zeros((TIME,), jnp.float32).at[1:RAMAN_TAPS + 1].set(kernel)
    spectrum = jnp.fft.fft(padded)
    frequency = jnp.arange(TIME, dtype=jnp.int32)
    norm_freq = jnp.where(frequency < TIME // 2, frequency, frequency - TIME).astype(jnp.float32) * (2.0 / TIME)
    phase = betas[:, 0:1] + betas[:, 1:2] * norm_freq + betas[:, 2:3] * (norm_freq * norm_freq) / 2.0 + betas[:, 3:4] * (norm_freq * norm_freq * norm_freq) / 6.0
    half_phase = phase * 0.5
    rotation = lax.complex(jnp.cos(half_phase), jnp.sin(half_phase))

    def disperse(real_part, imag_part):
        values = jnp.fft.ifft(jnp.fft.fft(lax.complex(real_part, imag_part), axis=1) * rotation, axis=1)
        return jnp.real(values), jnp.imag(values)

    block_len = GRID // N_MODE

    def nonlinear(real_part, imag_part):
        def one_block(running, block_no):
            profile = lax.dynamic_slice_in_dim(modes, block_no * block_len, block_len, 1)
            grid_real = jnp.dot(profile.T, real_part, precision=lax.Precision.HIGHEST)
            grid_imag = jnp.dot(profile.T, imag_part, precision=lax.Precision.HIGHEST)
            intensity = grid_real * grid_real + grid_imag * grid_imag
            delayed = jnp.real(jnp.fft.ifft(jnp.fft.fft(intensity, axis=1) * spectrum, axis=1))
            weight = (1.0 - RAMAN_SHARE) * intensity + RAMAN_SHARE * delayed
            resp_real = running[0] + jnp.dot(profile, grid_real * weight, precision=lax.Precision.HIGHEST)
            resp_imag = running[1] + jnp.dot(profile, grid_imag * weight, precision=lax.Precision.HIGHEST)
            return (resp_real, resp_imag), None

        empty_modes = jnp.zeros(real_part.shape, jnp.float32)
        response, unused = lax.scan(one_block, (empty_modes, empty_modes), jnp.arange(N_MODE, dtype=jnp.int32))
        return real_part - KERR_GAIN * response[1], imag_part + KERR_GAIN * response[0]

    real_part = field[:, 0, :]
    imag_part = field[:, 1, :]
    for number in range(ITERS):
        real_part, imag_part = disperse(real_part, imag_part)
        real_part, imag_part = nonlinear(real_part, imag_part)
        real_part, imag_part = disperse(real_part, imag_part)
    return jnp.stack([real_part, imag_part], 1)
```

```python
import math

import jax
import jax.numpy as jnp
import numpy as np
from jax import lax
from jax.sharding import PartitionSpec as P

RAMAN_TAPS = 256
ITERS = 2
RAMAN_SHARE = 0.18
KERR_GAIN = 6.0
PRECISE = lax.Precision.HIGHEST
BOTH = ("mode", "tm")


def exp_table(product, length):
    angle = (product % length) * (2.0 * math.pi / length)
    return np.cos(angle), np.sin(angle)


def block_matrix(cosine, sine):
    return np.stack([np.stack([cosine, -sine], 1), np.stack([sine, cosine], 1)], 0)


def raman_matrix(block, halo):
    positions = np.arange(1, RAMAN_TAPS + 1)
    spacing = 256.0 / RAMAN_TAPS
    raw = np.exp(-positions * spacing / 32.0) * np.sin(positions * spacing / 12.2)
    taps = raw / raw.sum()
    lag = np.arange(block)[None, :] + halo * block - np.arange((halo + 1) * block)[:, None]
    return np.where((lag >= 1) & (lag <= RAMAN_TAPS), taps[np.clip(lag, 1, RAMAN_TAPS) - 1], 0.0)


def general(field, modes, betas):
    n_mode, n_tm = lax.axis_size("mode"), lax.axis_size("tm")
    t_index = lax.axis_index("tm")
    own_modes, _, samples = field.shape
    n_dev = n_mode * n_tm
    total = samples * n_tm
    block = total // n_dev
    halo = -(-RAMAN_TAPS // block)
    rows = -(-own_modes // n_tm)
    spare = n_tm * rows - own_modes
    f32 = jnp.float32

    dev, pos = np.arange(n_dev), np.arange(block)
    cos_a, sin_a = exp_table(dev[:, None] * dev[None, :], n_dev)
    cos_t, sin_t = exp_table(dev[:, None] * pos[None, :], total)
    cos_b, sin_b = exp_table(pos[:, None] * pos[None, :], block)
    first = jnp.asarray(block_matrix(cos_a, sin_a), f32)
    first_back = jnp.asarray(block_matrix(cos_a, -sin_a) / total, f32)
    last = jnp.asarray(block_matrix(cos_b, sin_b), f32)
    last_back = jnp.asarray(block_matrix(cos_b, -sin_b), f32)
    twist = (jnp.asarray(cos_t, f32), jnp.asarray(sin_t, f32))

    frequency = dev[:, None] + n_dev * pos[None, :]
    norm_freq = jnp.asarray(np.where(frequency < total // 2, frequency, frequency - total) * (2.0 / total), f32)
    rates = lax.dynamic_slice_in_dim(jnp.pad(betas, ((0, spare), (0, 0))), t_index * rows, rows, 0)
    rates = rates[:, :, None, None]
    phase = (
        rates[:, 0]
        + rates[:, 1] * norm_freq
        + rates[:, 2] * (norm_freq * norm_freq) / 2.0
        + rates[:, 3] * (norm_freq * norm_freq * norm_freq) / 6.0
    )
    half_turn = (jnp.cos(phase * 0.5), jnp.sin(phase * 0.5))
    full_turn = (jnp.cos(phase), jnp.sin(phase))

    def disperse(blocks, turn):
        x = jnp.einsum("arcb,cadk->drkb", blocks, first, precision=PRECISE)
        x = jnp.stack([x[0] * twist[0] + x[1] * twist[1], x[1] * twist[0] - x[0] * twist[1]], 0)
        x = jnp.einsum("crkb,cbdq->drkq", x, last, precision=PRECISE)
        x = jnp.stack([x[0] * turn[0] - x[1] * turn[1], x[0] * turn[1] + x[1] * turn[0]], 0)
        x = jnp.einsum("crkq,cqdb->drkb", x, last_back, precision=PRECISE)
        x = jnp.stack([x[0] * twist[0] - x[1] * twist[1], x[1] * twist[0] + x[0] * twist[1]], 0)
        return jnp.einsum("crkb,ckda->ardb", x, first_back, precision=PRECISE)

    raman = jnp.asarray(raman_matrix(block, halo), f32)
    all_profiles = lax.all_gather(modes, "mode", axis=1, tiled=True)
    all_modes = n_mode * own_modes

    def nonlinear(blocks):
        windows = jnp.stack([jnp.roll(blocks, halo - h, axis=0) for h in range(halo + 1)], 3)
        windows = lax.all_to_all(windows, BOTH, 0, 0, tiled=True)
        windows = windows.reshape(n_mode, n_tm * rows, 2, (halo + 1) * block)[:, :own_modes]
        windows = windows.reshape(all_modes, 2, (halo + 1) * block)
        grid = jnp.einsum("pg,pct->cgt", all_profiles, windows, precision=PRECISE)
        intensity = grid[0] * grid[0] + grid[1] * grid[1]
        delayed = jnp.dot(intensity, raman, precision=PRECISE)
        own = slice(halo * block, None)
        weight = (1.0 - RAMAN_SHARE) * intensity[:, own] + RAMAN_SHARE * delayed
        response = jnp.einsum("pg,cgt->pct", all_profiles, grid[:, :, own] * weight, precision=PRECISE)
        values = jnp.stack(
            [
                windows[:, 0, own] - KERR_GAIN * response[:, 1],
                windows[:, 1, own] + KERR_GAIN * response[:, 0],
            ],
            1,
        )
        values = jnp.pad(values.reshape(n_mode, own_modes, 2, block), ((0, 0), (0, spare), (0, 0), (0, 0)))
        return lax.all_to_all(values.reshape(n_dev, rows, 2, block), BOTH, 0, 0, tiled=True)

    entry = jnp.pad(field, ((0, spare), (0, 0), (0, 0))).reshape(n_tm, rows, 2, samples)
    entry = lax.all_to_all(entry, "tm", 0, 0, tiled=True)
    per_tm = samples // block
    blocks = entry.reshape(n_tm, rows, 2, per_tm, block).transpose(0, 3, 1, 2, 4).reshape(n_dev, rows, 2, block)
    blocks = disperse(blocks, half_turn)
    for number in range(ITERS):
        blocks = nonlinear(blocks)
        blocks = disperse(blocks, full_turn if number < ITERS - 1 else half_turn)
    leave = blocks.reshape(n_tm, per_tm, rows, 2, block).transpose(0, 2, 3, 1, 4).reshape(n_tm, rows, 2, samples)
    leave = lax.all_to_all(leave, "tm", 0, 0, tiled=True)
    return leave.reshape(n_tm * rows, 2, samples)[:own_modes]


def solution(mesh):
    return jax.shard_map(
        general,
        mesh=mesh,
        in_specs=(P("mode", None, "tm"), P(None, "mode"), P("mode", None)),
        out_specs=P("mode", None, "tm"),
        check_vma=False,
    )
```

```python
import functools
import math

import jax
import jax.numpy as jnp
import numpy as np
from jax import lax
from jax.experimental import pallas as pl
from jax.experimental.pallas import tpu as pltpu
from jax.sharding import PartitionSpec as P


RAMAN_TAPS = 256
ITERS = 2
RAMAN_SHARE = 0.18
KERR_GAIN = 6.0
PRECISE = lax.Precision.HIGHEST
BOTH = ("mode", "tm")
PARAMS = pltpu.CompilerParams(vmem_limit_bytes=16 * 1024 * 1024)


def exp_table(product, length):
    angle = (product % length) * (2.0 * math.pi / length)
    return np.cos(angle), np.sin(angle)


def block_matrix(cosine, sine):
    return np.stack([np.stack([cosine, -sine], 1), np.stack([sine, cosine], 1)], 0)


def raman_matrix(block, halo):
    positions = np.arange(1, RAMAN_TAPS + 1)
    spacing = 256.0 / RAMAN_TAPS
    raw = np.exp(-positions * spacing / 32.0) * np.sin(positions * spacing / 12.2)
    taps = raw / raw.sum()
    lag = np.arange(block)[None, :] + halo * block - np.arange((halo + 1) * block)[:, None]
    return np.where((lag >= 1) & (lag <= RAMAN_TAPS), taps[np.clip(lag, 1, RAMAN_TAPS) - 1], 0.0)


def general(field, modes, betas):
    n_mode, n_tm = lax.axis_size("mode"), lax.axis_size("tm")
    t_index = lax.axis_index("tm")
    own_modes, _, samples = field.shape
    n_dev = n_mode * n_tm
    total = samples * n_tm
    block = total // n_dev
    halo = -(-RAMAN_TAPS // block)
    rows = -(-own_modes // n_tm)
    spare = n_tm * rows - own_modes
    f32 = jnp.float32

    dev, pos = np.arange(n_dev), np.arange(block)
    cos_a, sin_a = exp_table(dev[:, None] * dev[None, :], n_dev)
    cos_t, sin_t = exp_table(dev[:, None] * pos[None, :], total)
    cos_b, sin_b = exp_table(pos[:, None] * pos[None, :], block)
    first = jnp.asarray(block_matrix(cos_a, sin_a), f32)
    first_back = jnp.asarray(block_matrix(cos_a, -sin_a) / total, f32)
    last = jnp.asarray(block_matrix(cos_b, sin_b), f32)
    last_back = jnp.asarray(block_matrix(cos_b, -sin_b), f32)
    twist = (jnp.asarray(cos_t, f32), jnp.asarray(sin_t, f32))

    frequency = dev[:, None] + n_dev * pos[None, :]
    norm_freq = jnp.asarray(np.where(frequency < total // 2, frequency, frequency - total) * (2.0 / total), f32)
    rates = lax.dynamic_slice_in_dim(jnp.pad(betas, ((0, spare), (0, 0))), t_index * rows, rows, 0)
    rates = rates[:, :, None, None]
    phase = (
        rates[:, 0]
        + rates[:, 1] * norm_freq
        + rates[:, 2] * (norm_freq * norm_freq) / 2.0
        + rates[:, 3] * (norm_freq * norm_freq * norm_freq) / 6.0
    )
    half_turn = (jnp.cos(phase * 0.5), jnp.sin(phase * 0.5))
    full_turn = (jnp.cos(phase), jnp.sin(phase))

    def disperse(blocks, turn):
        x = jnp.einsum("arcb,cadk->drkb", blocks, first, precision=PRECISE)
        x = jnp.stack([x[0] * twist[0] + x[1] * twist[1], x[1] * twist[0] - x[0] * twist[1]], 0)
        x = jnp.einsum("crkb,cbdq->drkq", x, last, precision=PRECISE)
        x = jnp.stack([x[0] * turn[0] - x[1] * turn[1], x[0] * turn[1] + x[1] * turn[0]], 0)
        x = jnp.einsum("crkq,cqdb->drkb", x, last_back, precision=PRECISE)
        x = jnp.stack([x[0] * twist[0] - x[1] * twist[1], x[1] * twist[0] + x[0] * twist[1]], 0)
        return jnp.einsum("crkb,ckda->ardb", x, first_back, precision=PRECISE)

    raman = jnp.asarray(raman_matrix(block, halo), f32)
    all_profiles = lax.all_gather(modes, "mode", axis=1, tiled=True)
    all_modes = n_mode * own_modes

    def nonlinear(blocks):
        windows = jnp.stack([jnp.roll(blocks, halo - h, axis=0) for h in range(halo + 1)], 3)
        windows = lax.all_to_all(windows, BOTH, 0, 0, tiled=True)
        windows = windows.reshape(n_mode, n_tm * rows, 2, (halo + 1) * block)[:, :own_modes]
        windows = windows.reshape(all_modes, 2, (halo + 1) * block)
        grid = jnp.einsum("pg,pct->cgt", all_profiles, windows, precision=PRECISE)
        intensity = grid[0] * grid[0] + grid[1] * grid[1]
        delayed = jnp.dot(intensity, raman, precision=PRECISE)
        own = slice(halo * block, None)
        weight = (1.0 - RAMAN_SHARE) * intensity[:, own] + RAMAN_SHARE * delayed
        response = jnp.einsum("pg,cgt->pct", all_profiles, grid[:, :, own] * weight, precision=PRECISE)
        values = jnp.stack(
            [
                windows[:, 0, own] - KERR_GAIN * response[:, 1],
                windows[:, 1, own] + KERR_GAIN * response[:, 0],
            ],
            1,
        )
        values = jnp.pad(values.reshape(n_mode, own_modes, 2, block), ((0, 0), (0, spare), (0, 0), (0, 0)))
        return lax.all_to_all(values.reshape(n_dev, rows, 2, block), BOTH, 0, 0, tiled=True)

    entry = jnp.pad(field, ((0, spare), (0, 0), (0, 0))).reshape(n_tm, rows, 2, samples)
    entry = lax.all_to_all(entry, "tm", 0, 0, tiled=True)
    per_tm = samples // block
    blocks = entry.reshape(n_tm, rows, 2, per_tm, block).transpose(0, 3, 1, 2, 4).reshape(n_dev, rows, 2, block)
    blocks = disperse(blocks, half_turn)
    for number in range(ITERS):
        blocks = nonlinear(blocks)
        blocks = disperse(blocks, full_turn if number < ITERS - 1 else half_turn)
    leave = blocks.reshape(n_tm, per_tm, rows, 2, block).transpose(0, 2, 3, 1, 4).reshape(n_tm, rows, 2, samples)
    leave = lax.all_to_all(leave, "tm", 0, 0, tiled=True)
    return leave.reshape(n_tm * rows, 2, samples)[:own_modes]


def split_two(values):
    high = values.astype(jnp.bfloat16)
    return high, (values - high.astype(jnp.float32)).astype(jnp.bfloat16)


def np_split(values):
    high = values.astype(jnp.bfloat16)
    return high, (values - high.astype(np.float64)).astype(jnp.bfloat16)


def product(left, right):
    return jnp.dot(left, right, preferred_element_type=jnp.float32)


def turn_kernel(scale, rates_ref, freq_ref, half_ref, full_ref):
    freq = freq_ref[...]
    square = freq * freq
    size = freq.shape[0]
    for r in range(rates_ref.shape[0]):
        phase = (
            rates_ref[r, 0]
            + rates_ref[r, 1] * freq
            + rates_ref[r, 2] * square / 2.0
            + rates_ref[r, 3] * (square * freq) / 6.0
        )
        cosine, sine = jnp.cos(phase * 0.5), jnp.sin(phase * 0.5)
        part = pl.ds(r * size, size)
        half_ref[0, part] = cosine * scale
        half_ref[1, part] = sine * scale
        full_ref[0, part] = (cosine * cosine - sine * sine) * scale
        full_ref[1, part] = (2.0 * scale) * cosine * sine


def disperse_kernel(rows, load, store, x_ref, first_ref, last_ref, twist_ref, turn_ref, final_ref, o_ref):
    n_dev, block = twist_ref.shape[1:]
    width = 2 * block
    twist = [jnp.concatenate([twist_ref[c]] * rows, axis=1) for c in range(2)]

    def across(matrix_ref, values):
        high, low = split_two(values)
        return product(matrix_ref[...], jnp.concatenate([high, high, low, low], axis=0))

    def twisted(values):
        re, im = values[:n_dev], values[n_dev:]
        return re * twist[0] + im * twist[1], im * twist[0] - re * twist[1]

    def along(re, im):
        high, low = split_two(jnp.concatenate([re, im], axis=1))
        both = product(jnp.concatenate([high, low], axis=0), last_ref[:, :width])
        size = high.shape[0]
        return both[:size] + both[size:] + product(high, last_ref[:, width:])

    def row_of(values):
        return jnp.concatenate([values[:, r * block : (r + 1) * block] for r in range(rows)], axis=0)

    def lane_of(values):
        return jnp.concatenate([values[r * n_dev : (r + 1) * n_dev] for r in range(rows)], axis=1)

    x = jnp.concatenate(
        [jnp.concatenate([load(x_ref, r, c) for r in range(rows)], axis=1) for c in range(2)], axis=0
    )
    re, im = twisted(across(first_ref, x))
    z = along(row_of(re), row_of(im))
    z_re, z_im = z[:, :block], z[:, block:]
    turn_re, turn_im = turn_ref[0], turn_ref[1]
    z = along(z_re * turn_re - z_im * turn_im, -(z_re * turn_im + z_im * turn_re))
    re, im = twisted(jnp.concatenate([lane_of(z[:, :block]), lane_of(z[:, block:])], axis=0))
    x = across(final_ref, jnp.concatenate([re, im], axis=0))
    for r in range(rows):
        lanes = slice(r * block, (r + 1) * block)
        store(o_ref, r, 0, x[:n_dev, lanes])
        store(o_ref, r, 1, -x[n_dev:, lanes])


def nonlinear_kernel(rows, halo, step, w_ref, up_ref, down_ref, raman_ref, o_ref):
    block = w_ref.shape[1]
    span = (halo + 1) * block
    n_dev = w_ref.shape[0] // ((halo + 1) * rows * 2)
    n_modes = n_dev * rows
    n_grid = up_ref.shape[0]
    chunk = (halo + 1) * rows * 2

    def window(c):
        return jnp.concatenate(
            [
                jnp.concatenate(
                    [w_ref[pl.ds(h * 2 * rows + 2 * r + c, n_dev, stride=chunk), :] for r in range(rows)], axis=0
                )
                for h in range(halo + 1)
            ],
            axis=1,
        )

    values = [window(0), window(1)]
    high, low = split_two(jnp.concatenate(values, axis=1))
    high = jnp.concatenate([high, high], axis=0)
    low = jnp.concatenate([low, low], axis=0)
    response = None
    for start in range(0, n_grid, step):
        up = up_ref[start : start + step, :]
        grid = product(up, low) + product(up, high)
        g_re, g_im = grid[:, :span], grid[:, span:]
        intensity = g_re * g_re + g_im * g_im
        i_high, i_low = split_two(intensity)
        both = product(i_high, raman_ref[...])
        delayed = both[:, :block] + both[:, block:] + product(i_low, raman_ref[:, :block])
        weight = (1.0 - RAMAN_SHARE) * intensity[:, halo * block :] + delayed
        drive = jnp.concatenate([g_re[:, halo * block :] * weight, g_im[:, halo * block :] * weight], axis=1)
        d_high, d_low = split_two(drive)
        both = product(down_ref[:, start : start + step], d_high)
        part = both[:n_modes] + both[n_modes:] + product(down_ref[:n_modes, start : start + step], d_low)
        response = part if response is None else response + part
    out = [
        values[0][:, halo * block :] - KERR_GAIN * response[:, block:],
        values[1][:, halo * block :] + KERR_GAIN * response[:, :block],
    ]
    for c in range(2):
        for r in range(rows):
            o_ref[pl.ds(2 * r + c, n_dev, stride=2 * rows), :] = out[c][r * n_dev : (r + 1) * n_dev]


def tiled(field, modes, betas):
    n_mode, n_tm = lax.axis_size("mode"), lax.axis_size("tm")
    t_index = lax.axis_index("tm")
    own_modes, _, samples = field.shape
    n_dev = n_mode * n_tm
    total = samples * n_tm
    block = total // n_dev
    halo = -(-RAMAN_TAPS // block)
    rows = own_modes // n_tm
    per_tm = samples // block
    f32 = jnp.float32

    pieces = [modes]
    for shift in range(1, n_mode):
        pieces.append(lax.ppermute(modes, "mode", [(i, (i + shift) % n_mode) for i in range(n_mode)]))
    profiles = jnp.concatenate(pieces, axis=1)
    profiles = profiles.reshape(n_dev, rows, -1).transpose(1, 0, 2).reshape(n_dev * rows, -1)
    high = lax.reduce_precision(profiles, 8, 7)
    low = profiles - high
    down = jnp.concatenate([high, low], axis=0).astype(jnp.bfloat16)
    up = down.T

    dev, pos = np.arange(n_dev), np.arange(block)
    cos_a, sin_a = exp_table(dev[:, None] * dev[None, :], n_dev)
    cos_t, sin_t = exp_table(dev[:, None] * pos[None, :], total)
    cos_b, sin_b = exp_table(pos[:, None] * pos[None, :], block)
    first = block_matrix(cos_a, sin_a).transpose(2, 3, 0, 1)
    last = block_matrix(cos_b, sin_b).reshape(2 * block, 2 * block)
    last = jnp.asarray(np.concatenate(np_split(last), axis=1))
    twist = jnp.asarray(np.stack([cos_t, sin_t]), f32)
    edge = np.arange(n_dev).reshape(n_tm, per_tm).T.reshape(-1)

    def flat(matrix):
        high, low = np_split(matrix.reshape(2 * n_dev, 2 * n_dev))
        return jnp.asarray(np.concatenate([high, low, high, low], axis=1))

    frequency = dev[:, None] + n_dev * pos[None, :]
    norm_freq = jnp.asarray(np.where(frequency < total // 2, frequency, frequency - total) * (2.0 / total), f32)
    rates = lax.dynamic_slice_in_dim(betas, t_index * rows, rows, 0)
    table = jax.ShapeDtypeStruct((2, rows * n_dev, block), f32)
    half_turn, full_turn = pl.pallas_call(
        functools.partial(turn_kernel, 1.0 / total),
        out_shape=(table, table),
        in_specs=[pl.BlockSpec(memory_space=pltpu.SMEM), pl.BlockSpec(memory_space=pltpu.VMEM)],
        name="turns",
        compiler_params=PARAMS,
    )(rates, norm_freq)

    def load_edge(ref, r, c):
        return jnp.concatenate([ref[:, r, c, q * block : (q + 1) * block] for q in range(per_tm)], axis=0)

    def load_inner(ref, r, c):
        return ref[pl.ds(2 * r + c, n_dev, stride=2 * rows), :]

    def store_edge(ref, r, c, values):
        for q in range(per_tm):
            ref[:, r, c, q * block : (q + 1) * block] = values[q * n_tm : (q + 1) * n_tm]

    def store_inner(ref, r, c, values):
        for h in range(halo + 1):
            moved = pltpu.roll(values, halo - h, axis=0) if h < halo else values
            ref[pl.ds(2 * (h * rows + r) + c, n_dev, stride=2 * (halo + 1) * rows), :] = moved

    def disperse(values, turn, entering, leaving):
        shape = (n_tm, rows, 2, samples) if leaving else (n_dev * (halo + 1) * rows * 2, block)
        return pl.pallas_call(
            functools.partial(
                disperse_kernel,
                rows,
                load_edge if entering else load_inner,
                store_edge if leaving else store_inner,
            ),
            out_shape=jax.ShapeDtypeStruct(shape, f32),
            name="disperse",
            compiler_params=PARAMS,
        )(
            values,
            flat(first[..., edge] if entering else first),
            last,
            twist,
            turn,
            flat(first[:, edge] if leaving else first),
        )

    taps = RAMAN_SHARE * raman_matrix(block, halo)
    raman = jnp.asarray(np.concatenate(np_split(taps), axis=1))
    step = math.gcd(up.shape[0], 256)

    def nonlinear(windows):
        return pl.pallas_call(
            functools.partial(nonlinear_kernel, rows, halo, step),
            out_shape=jax.ShapeDtypeStruct((n_dev * rows * 2, block), f32),
            name="nonlinear",
            compiler_params=PARAMS,
        )(windows, up, down, raman)

    def exchange(values):
        shaped = values.reshape(n_dev, -1, 2, block)
        return lax.all_to_all(shaped, BOTH, 0, 0, tiled=True).reshape(-1, block)

    values = lax.all_to_all(field.reshape(n_tm, rows, 2, samples), "tm", 0, 0, tiled=True)
    values = disperse(values, half_turn, True, False)
    for number in range(ITERS):
        values = exchange(values)
        values = nonlinear(values)
        leaving = number == ITERS - 1
        values = disperse(exchange(values), half_turn if leaving else full_turn, False, leaving)
    return lax.all_to_all(values, "tm", 0, 0, tiled=True).reshape(field.shape)


def shards(field, modes, betas):
    n_mode, n_tm = lax.axis_size("mode"), lax.axis_size("tm")
    fits = (
        field.shape[2] % (128 * n_mode) == 0
        and field.shape[0] % n_tm == 0
        and n_tm % 8 == 0
        and modes.shape[1] % 128 == 0
    )
    if not fits:
        return general(field, modes, betas)
    return tiled(field, modes, betas)


def solution(mesh):
    return jax.shard_map(
        shards,
        mesh=mesh,
        in_specs=(P("mode", None, "tm"), P(None, "mode"), P("mode", None)),
        out_specs=P("mode", None, "tm"),
        check_vma=False,
    )
```

```python
import functools
import math

import jax
import jax.numpy as jnp
import numpy as np
from jax import lax
from jax.experimental import pallas as pl
from jax.experimental.layout import Layout, with_layout_constraint
from jax.experimental.pallas import tpu as pltpu
from jax.sharding import PartitionSpec as P


RAMAN_TAPS = 256
ITERS = 2
RAMAN_SHARE = 0.18
KERR_GAIN = 6.0
PRECISE = lax.Precision.HIGHEST
BOTH = ("mode", "tm")
PARAMS = pltpu.CompilerParams(vmem_limit_bytes=16 * 1024 * 1024)


def exp_table(product, length):
    angle = (product % length) * (2.0 * math.pi / length)
    return np.cos(angle), np.sin(angle)


def block_matrix(cosine, sine):
    return np.stack([np.stack([cosine, -sine], 1), np.stack([sine, cosine], 1)], 0)


def raman_taps():
    positions = np.arange(1, RAMAN_TAPS + 1)
    spacing = 256.0 / RAMAN_TAPS
    raw = np.exp(-positions * spacing / 32.0) * np.sin(positions * spacing / 12.2)
    return raw / raw.sum()


def raman_matrix(block, halo):
    taps = raman_taps()
    lag = np.arange(block)[None, :] + halo * block - np.arange((halo + 1) * block)[:, None]
    return np.where((lag >= 1) & (lag <= RAMAN_TAPS), taps[np.clip(lag, 1, RAMAN_TAPS) - 1], 0.0)


def general(field, modes, betas):
    n_mode, n_tm = lax.axis_size("mode"), lax.axis_size("tm")
    t_index = lax.axis_index("tm")
    own_modes, _, samples = field.shape
    n_dev = n_mode * n_tm
    total = samples * n_tm
    block = total // n_dev
    halo = -(-RAMAN_TAPS // block)
    rows = -(-own_modes // n_tm)
    spare = n_tm * rows - own_modes
    f32 = jnp.float32

    dev, pos = np.arange(n_dev), np.arange(block)
    cos_a, sin_a = exp_table(dev[:, None] * dev[None, :], n_dev)
    cos_t, sin_t = exp_table(dev[:, None] * pos[None, :], total)
    cos_b, sin_b = exp_table(pos[:, None] * pos[None, :], block)
    first = jnp.asarray(block_matrix(cos_a, sin_a), f32)
    first_back = jnp.asarray(block_matrix(cos_a, -sin_a) / total, f32)
    last = jnp.asarray(block_matrix(cos_b, sin_b), f32)
    last_back = jnp.asarray(block_matrix(cos_b, -sin_b), f32)
    twist = (jnp.asarray(cos_t, f32), jnp.asarray(sin_t, f32))

    frequency = dev[:, None] + n_dev * pos[None, :]
    norm_freq = jnp.asarray(np.where(frequency < total // 2, frequency, frequency - total) * (2.0 / total), f32)
    rates = lax.dynamic_slice_in_dim(jnp.pad(betas, ((0, spare), (0, 0))), t_index * rows, rows, 0)
    rates = rates[:, :, None, None]
    phase = (
        rates[:, 0]
        + rates[:, 1] * norm_freq
        + rates[:, 2] * (norm_freq * norm_freq) / 2.0
        + rates[:, 3] * (norm_freq * norm_freq * norm_freq) / 6.0
    )
    half_turn = (jnp.cos(phase * 0.5), jnp.sin(phase * 0.5))
    full_turn = (jnp.cos(phase), jnp.sin(phase))

    def disperse(blocks, turn):
        x = jnp.einsum("arcb,cadk->drkb", blocks, first, precision=PRECISE)
        x = jnp.stack([x[0] * twist[0] + x[1] * twist[1], x[1] * twist[0] - x[0] * twist[1]], 0)
        x = jnp.einsum("crkb,cbdq->drkq", x, last, precision=PRECISE)
        x = jnp.stack([x[0] * turn[0] - x[1] * turn[1], x[0] * turn[1] + x[1] * turn[0]], 0)
        x = jnp.einsum("crkq,cqdb->drkb", x, last_back, precision=PRECISE)
        x = jnp.stack([x[0] * twist[0] - x[1] * twist[1], x[1] * twist[0] + x[0] * twist[1]], 0)
        return jnp.einsum("crkb,ckda->ardb", x, first_back, precision=PRECISE)

    raman = jnp.asarray(raman_matrix(block, halo), f32)
    all_profiles = lax.all_gather(modes, "mode", axis=1, tiled=True)
    all_modes = n_mode * own_modes

    def nonlinear(blocks):
        windows = jnp.stack([jnp.roll(blocks, halo - h, axis=0) for h in range(halo + 1)], 3)
        windows = lax.all_to_all(windows, BOTH, 0, 0, tiled=True)
        windows = windows.reshape(n_mode, n_tm * rows, 2, (halo + 1) * block)[:, :own_modes]
        windows = windows.reshape(all_modes, 2, (halo + 1) * block)
        grid = jnp.einsum("pg,pct->cgt", all_profiles, windows, precision=PRECISE)
        intensity = grid[0] * grid[0] + grid[1] * grid[1]
        delayed = jnp.dot(intensity, raman, precision=PRECISE)
        own = slice(halo * block, None)
        weight = (1.0 - RAMAN_SHARE) * intensity[:, own] + RAMAN_SHARE * delayed
        response = jnp.einsum("pg,cgt->pct", all_profiles, grid[:, :, own] * weight, precision=PRECISE)
        values = jnp.stack(
            [
                windows[:, 0, own] - KERR_GAIN * response[:, 1],
                windows[:, 1, own] + KERR_GAIN * response[:, 0],
            ],
            1,
        )
        values = jnp.pad(values.reshape(n_mode, own_modes, 2, block), ((0, 0), (0, spare), (0, 0), (0, 0)))
        return lax.all_to_all(values.reshape(n_dev, rows, 2, block), BOTH, 0, 0, tiled=True)

    entry = jnp.pad(field, ((0, spare), (0, 0), (0, 0))).reshape(n_tm, rows, 2, samples)
    entry = lax.all_to_all(entry, "tm", 0, 0, tiled=True)
    per_tm = samples // block
    blocks = entry.reshape(n_tm, rows, 2, per_tm, block).transpose(0, 3, 1, 2, 4).reshape(n_dev, rows, 2, block)
    blocks = disperse(blocks, half_turn)
    for number in range(ITERS):
        blocks = nonlinear(blocks)
        blocks = disperse(blocks, full_turn if number < ITERS - 1 else half_turn)
    leave = blocks.reshape(n_tm, per_tm, rows, 2, block).transpose(0, 2, 3, 1, 4).reshape(n_tm, rows, 2, samples)
    leave = lax.all_to_all(leave, "tm", 0, 0, tiled=True)
    return leave.reshape(n_tm * rows, 2, samples)[:own_modes]


def split_two(values):
    high = values.astype(jnp.bfloat16)
    return high, (values - high.astype(jnp.float32)).astype(jnp.bfloat16)


def np_split(values):
    high = values.astype(jnp.bfloat16)
    return high, (values - high.astype(np.float64)).astype(jnp.bfloat16)


def product(left, right):
    return jnp.dot(left, right, preferred_element_type=jnp.float32)


def turn_kernel(scale, rates_ref, freq_ref, taps_ref, half_ref, full_ref, raman_ref):
    window, double = raman_ref.shape
    block = double // 2
    taps = jnp.broadcast_to(taps_ref[0:1, :], (window, taps_ref.shape[1]))
    taps = pltpu.roll(taps, block, axis=1, stride=1, stride_axis=0)[:, :block]
    raman_ref[...] = jnp.concatenate(split_two(taps), axis=1)
    freq = freq_ref[...]
    square = freq * freq
    size = freq.shape[0]
    for r in range(rates_ref.shape[0]):
        phase = (
            rates_ref[r, 0]
            + rates_ref[r, 1] * freq
            + rates_ref[r, 2] * square / 2.0
            + rates_ref[r, 3] * (square * freq) / 6.0
        )
        cosine, sine = jnp.cos(phase * 0.5), jnp.sin(phase * 0.5)
        part = pl.ds(r * size, size)
        half_ref[0, part] = cosine * scale
        half_ref[1, part] = sine * scale
        full_ref[0, part] = (cosine * cosine - sine * sine) * scale
        full_ref[1, part] = (2.0 * scale) * cosine * sine


def profile_kernel(rows, *refs):
    pieces, (up_ref, down_ref) = refs[:-3], refs[-2:]
    count = pieces[0].shape[0]
    n_dev = count // rows
    place, mode = (lax.broadcasted_iota(jnp.int32, (count, count), d) for d in range(2))
    order = (mode == (place % n_dev) * rows + place // n_dev).astype(jnp.float32).astype(jnp.bfloat16)
    start = 0
    for piece in pieces:
        width = piece.shape[1]
        wide, low = (product(order, part) for part in split_two(piece[...]))
        down_ref[:, start : start + width] = jnp.concatenate([wide, low], axis=0).astype(jnp.bfloat16)
        stack = jnp.concatenate([wide, low, wide, low], axis=0)
        up_ref[start : start + width, :] = stack.T.astype(jnp.bfloat16)
        start += width


def disperse_kernel(rows, load, store, x_ref, first_ref, last_ref, twist_ref, turn_ref, o_ref):
    n_dev, block = twist_ref.shape[1:]
    cos_high, sin_high, cos_low, sin_low = (last_ref[:, n * block : (n + 1) * block] for n in range(4))
    last_high = jnp.concatenate(
        [jnp.concatenate([cos_high, -sin_high], axis=1), jnp.concatenate([sin_high, cos_high], axis=1)], axis=0
    )
    last_low = jnp.concatenate(
        [jnp.concatenate([cos_low, -sin_low], axis=1), jnp.concatenate([sin_low, cos_low], axis=1)], axis=0
    )
    twist = [jnp.concatenate([twist_ref[c]] * rows, axis=1) for c in range(2)]

    def across(place, values):
        high, low = split_two(values)
        return product(first_ref[place], jnp.concatenate([high, high, low, low], axis=0))

    def twisted(values):
        re, im = values[:n_dev], values[n_dev:]
        return re * twist[0] + im * twist[1], im * twist[0] - re * twist[1]

    def along(re, im):
        high, low = split_two(jnp.concatenate([re, im], axis=1))
        both = product(jnp.concatenate([high, low], axis=0), last_high)
        size = high.shape[0]
        return both[:size] + both[size:] + product(high, last_low)

    def row_of(values):
        return jnp.concatenate([values[:, r * block : (r + 1) * block] for r in range(rows)], axis=0)

    def lane_of(values):
        return jnp.concatenate([values[r * n_dev : (r + 1) * n_dev] for r in range(rows)], axis=1)

    x = jnp.concatenate(
        [jnp.concatenate([load(x_ref, r, c) for r in range(rows)], axis=1) for c in range(2)], axis=0
    )
    re, im = twisted(across(0, x))
    z = along(row_of(re), row_of(im))
    z_re, z_im = z[:, :block], z[:, block:]
    turn_re, turn_im = turn_ref[0], turn_ref[1]
    z = along(z_re * turn_re - z_im * turn_im, -(z_re * turn_im + z_im * turn_re))
    re, im = twisted(jnp.concatenate([lane_of(z[:, :block]), lane_of(z[:, block:])], axis=0))
    x = across(1, jnp.concatenate([re, im], axis=0))
    for r in range(rows):
        lanes = slice(r * block, (r + 1) * block)
        store(o_ref, r, 0, x[:n_dev, lanes])
        store(o_ref, r, 1, -x[n_dev:, lanes])


def nonlinear_kernel(rows, halo, step, w_ref, up_ref, down_ref, raman_ref, o_ref):
    block = w_ref.shape[1]
    span = (halo + 1) * block
    n_dev = w_ref.shape[0] // ((halo + 1) * rows * 2)
    n_modes = n_dev * rows
    n_grid = up_ref.shape[0]
    chunk = (halo + 1) * rows * 2

    def window(c):
        return jnp.concatenate(
            [
                jnp.concatenate(
                    [w_ref[pl.ds(h * 2 * rows + 2 * r + c, n_dev, stride=chunk), :] for r in range(rows)], axis=0
                )
                for h in range(halo + 1)
            ],
            axis=1,
        )

    taps = raman_ref[...]
    taps = jnp.concatenate(
        [taps, jnp.concatenate([taps[:, :block], jnp.zeros_like(taps[:, :block])], axis=1)], axis=0
    )
    values = [window(0), window(1)]
    high, low = split_two(jnp.concatenate(values, axis=1))
    fields = jnp.concatenate([high, high, low, low], axis=0)
    response = None
    for start in range(0, n_grid, step):
        up = up_ref[start : start + step, :]
        grid = product(up, fields)
        g_re, g_im = grid[:, :span], grid[:, span:]
        intensity = g_re * g_re + g_im * g_im
        i_high, i_low = split_two(intensity)
        both = product(jnp.concatenate([i_high, i_low], axis=1), taps)
        delayed = both[:, :block] + both[:, block:]
        weight = (1.0 - RAMAN_SHARE) * intensity[:, halo * block :] + delayed
        drive = jnp.concatenate([g_re[:, halo * block :] * weight, g_im[:, halo * block :] * weight], axis=1)
        d_high, d_low = split_two(drive)
        both = product(down_ref[:, start : start + step], d_high)
        part = both[:n_modes] + both[n_modes:] + product(down_ref[:n_modes, start : start + step], d_low)
        response = part if response is None else response + part
    out = [
        values[0][:, halo * block :] - KERR_GAIN * response[:, block:],
        values[1][:, halo * block :] + KERR_GAIN * response[:, :block],
    ]
    for c in range(2):
        for r in range(rows):
            o_ref[pl.ds(2 * r + c, n_dev, stride=2 * rows), :] = out[c][r * n_dev : (r + 1) * n_dev]


def tiled(field, modes, betas):
    n_mode, n_tm = lax.axis_size("mode"), lax.axis_size("tm")
    t_index = lax.axis_index("tm")
    own_modes, _, samples = field.shape
    n_dev = n_mode * n_tm
    total = samples * n_tm
    block = total // n_dev
    halo = -(-RAMAN_TAPS // block)
    rows = own_modes // n_tm
    per_tm = samples // block
    f32 = jnp.float32

    pieces = [modes]
    for shift in range(1, n_mode):
        pieces.append(lax.ppermute(modes, "mode", [(i, (i + shift) % n_mode) for i in range(n_mode)]))
    dev, pos = np.arange(n_dev), np.arange(block)
    cos_a, sin_a = exp_table(dev[:, None] * dev[None, :], n_dev)
    cos_t, sin_t = exp_table(dev[:, None] * pos[None, :], total)
    cos_b, sin_b = exp_table(pos[:, None] * pos[None, :], block)
    first = block_matrix(cos_a, sin_a).transpose(2, 3, 0, 1)
    (cos_high, cos_low), (sin_high, sin_low) = np_split(cos_b), np_split(sin_b)
    last = jnp.asarray(np.concatenate([cos_high, sin_high, cos_low, sin_low], axis=1))
    twist = jnp.asarray(np.stack([cos_t, sin_t]), f32)
    edge = np.arange(n_dev).reshape(n_tm, per_tm).T.reshape(-1)

    def flat(matrix):
        high, low = np_split(matrix.reshape(2 * n_dev, 2 * n_dev))
        return np.concatenate([high, low, high, low], axis=1)

    span = (halo + 1) * block
    lags = np.zeros((8, span + block))
    lags[:, block + 1 : block + 1 + RAMAN_TAPS] = RAMAN_SHARE * raman_taps()

    frequency = dev[:, None] + n_dev * pos[None, :]
    norm_freq = jnp.asarray(np.where(frequency < total // 2, frequency, frequency - total) * (2.0 / total), f32)
    rates = lax.dynamic_slice_in_dim(betas, t_index * rows, rows, 0)
    table = jax.ShapeDtypeStruct((2, rows * n_dev, block), f32)
    half_turn, full_turn, raman = pl.pallas_call(
        functools.partial(turn_kernel, 1.0 / total),
        out_shape=(table, table, jax.ShapeDtypeStruct((span, 2 * block), jnp.bfloat16)),
        in_specs=[pl.BlockSpec(memory_space=pltpu.SMEM)] + [pl.BlockSpec(memory_space=pltpu.VMEM)] * 2,
        name="turns",
        compiler_params=PARAMS,
    )(rates, norm_freq, jnp.asarray(lags, f32))

    def load_edge(ref, r, c):
        return jnp.concatenate(
            [
                ref[pl.ds(2 * (per_tm * r + q) + c, n_tm, stride=2 * per_tm * rows), :]
                for q in range(per_tm)
            ],
            axis=0,
        )

    def load_inner(ref, r, c):
        return ref[pl.ds(2 * r + c, n_dev, stride=2 * rows), :]

    def store_edge(ref, r, c, values):
        for q in range(per_tm):
            ref[:, r, c, q * block : (q + 1) * block] = values[q * n_tm : (q + 1) * n_tm]

    def store_inner(ref, r, c, values):
        for h in range(halo + 1):
            moved = pltpu.roll(values, halo - h, axis=0) if h < halo else values
            ref[pl.ds(2 * (h * rows + r) + c, n_dev, stride=2 * (halo + 1) * rows), :] = moved

    def disperse(values, turn, entering, leaving):
        shape = (n_tm, rows, 2, samples) if leaving else (n_dev * (halo + 1) * rows * 2, block)
        return pl.pallas_call(
            functools.partial(
                disperse_kernel,
                rows,
                load_edge if entering else load_inner,
                store_edge if leaving else store_inner,
            ),
            out_shape=jax.ShapeDtypeStruct(shape, f32),
            name="disperse",
            compiler_params=PARAMS,
        )(
            values,
            jnp.asarray(np.stack([flat(first[..., edge] if entering else first), flat(first[:, edge] if leaving else first)])),
            last,
            twist,
            turn,
        )

    def spread_profiles(windows):
        total_grid = modes.shape[1] * n_mode
        return pl.pallas_call(
            functools.partial(profile_kernel, rows),
            out_shape=(
                jax.ShapeDtypeStruct((total_grid, 4 * n_dev * rows), jnp.bfloat16),
                jax.ShapeDtypeStruct((2 * n_dev * rows, total_grid), jnp.bfloat16),
            ),
            in_specs=[pl.BlockSpec(memory_space=pltpu.VMEM)] * n_mode + [pl.BlockSpec(memory_space=pl.ANY)],
            name="profiles",
            compiler_params=PARAMS,
        )(*pieces, windows)

    step = math.gcd(modes.shape[1] * n_mode, 512)

    def nonlinear(windows, up, down):
        return pl.pallas_call(
            functools.partial(nonlinear_kernel, rows, halo, step),
            out_shape=jax.ShapeDtypeStruct((n_dev * rows * 2, block), f32),
            name="nonlinear",
            compiler_params=PARAMS,
        )(windows, up, down, raman)

    def exchange(values):
        shaped = values.reshape(n_dev, -1, 2, block)
        return lax.all_to_all(shaped, BOTH, 0, 0, tiled=True).reshape(-1, block)

    entry = field.reshape(own_modes, 2, per_tm, block)
    entry = with_layout_constraint(entry, Layout((0, 2, 1, 3)))
    entry = entry.transpose(0, 2, 1, 3).reshape(n_tm, rows * per_tm, 2, block)
    values = lax.all_to_all(entry, "tm", 0, 0, tiled=True).reshape(-1, block)
    values = disperse(values, half_turn, True, False)
    for number in range(ITERS):
        values = exchange(values)
        if number == 0:
            up, down = spread_profiles(values)
        values = nonlinear(values, up, down)
        leaving = number == ITERS - 1
        values = disperse(exchange(values), half_turn if leaving else full_turn, False, leaving)
    return lax.all_to_all(values, "tm", 0, 0, tiled=True).reshape(field.shape)


def shards(field, modes, betas):
    n_mode, n_tm = lax.axis_size("mode"), lax.axis_size("tm")
    fits = (
        field.shape[2] % (128 * n_mode) == 0
        and field.shape[0] % n_tm == 0
        and n_tm % 8 == 0
        and modes.shape[1] % 128 == 0
    )
    if not fits:
        return general(field, modes, betas)
    return tiled(field, modes, betas)


def solution(mesh):
    return jax.shard_map(
        shards,
        mesh=mesh,
        in_specs=(P("mode", None, "tm"), P(None, "mode"), P("mode", None)),
        out_specs=P("mode", None, "tm"),
        check_vma=False,
    )
```

```python
import functools
import math

import jax
import jax.numpy as jnp
import numpy as np
from jax import lax
from jax.experimental import pallas as pl
from jax.experimental.layout import Layout, with_layout_constraint
from jax.experimental.pallas import tpu as pltpu
from jax.sharding import PartitionSpec as P


RAMAN_TAPS = 256
ITERS = 2
RAMAN_SHARE = 0.18
KERR_GAIN = 6.0
PRECISE = lax.Precision.HIGHEST
BOTH = ("mode", "tm")
PARAMS = pltpu.CompilerParams(vmem_limit_bytes=16 * 1024 * 1024)


def exp_table(product, length):
    angle = (product % length) * (2.0 * math.pi / length)
    return np.cos(angle), np.sin(angle)


def block_matrix(cosine, sine):
    return np.stack([np.stack([cosine, -sine], 1), np.stack([sine, cosine], 1)], 0)


def raman_taps():
    positions = np.arange(1, RAMAN_TAPS + 1)
    spacing = 256.0 / RAMAN_TAPS
    raw = np.exp(-positions * spacing / 32.0) * np.sin(positions * spacing / 12.2)
    return raw / raw.sum()


def raman_matrix(block, halo):
    taps = raman_taps()
    lag = np.arange(block)[None, :] + halo * block - np.arange((halo + 1) * block)[:, None]
    return np.where((lag >= 1) & (lag <= RAMAN_TAPS), taps[np.clip(lag, 1, RAMAN_TAPS) - 1], 0.0)


def general(field, modes, betas):
    n_mode, n_tm = lax.axis_size("mode"), lax.axis_size("tm")
    t_index = lax.axis_index("tm")
    own_modes, _, samples = field.shape
    n_dev = n_mode * n_tm
    total = samples * n_tm
    block = total // n_dev
    halo = -(-RAMAN_TAPS // block)
    rows = -(-own_modes // n_tm)
    spare = n_tm * rows - own_modes
    f32 = jnp.float32

    dev, pos = np.arange(n_dev), np.arange(block)
    cos_a, sin_a = exp_table(dev[:, None] * dev[None, :], n_dev)
    cos_t, sin_t = exp_table(dev[:, None] * pos[None, :], total)
    cos_b, sin_b = exp_table(pos[:, None] * pos[None, :], block)
    first = jnp.asarray(block_matrix(cos_a, sin_a), f32)
    first_back = jnp.asarray(block_matrix(cos_a, -sin_a) / total, f32)
    last = jnp.asarray(block_matrix(cos_b, sin_b), f32)
    last_back = jnp.asarray(block_matrix(cos_b, -sin_b), f32)
    twist = (jnp.asarray(cos_t, f32), jnp.asarray(sin_t, f32))

    frequency = dev[:, None] + n_dev * pos[None, :]
    norm_freq = jnp.asarray(np.where(frequency < total // 2, frequency, frequency - total) * (2.0 / total), f32)
    rates = lax.dynamic_slice_in_dim(jnp.pad(betas, ((0, spare), (0, 0))), t_index * rows, rows, 0)
    rates = rates[:, :, None, None]
    phase = (
        rates[:, 0]
        + rates[:, 1] * norm_freq
        + rates[:, 2] * (norm_freq * norm_freq) / 2.0
        + rates[:, 3] * (norm_freq * norm_freq * norm_freq) / 6.0
    )
    half_turn = (jnp.cos(phase * 0.5), jnp.sin(phase * 0.5))
    full_turn = (jnp.cos(phase), jnp.sin(phase))

    def disperse(blocks, turn):
        x = jnp.einsum("arcb,cadk->drkb", blocks, first, precision=PRECISE)
        x = jnp.stack([x[0] * twist[0] + x[1] * twist[1], x[1] * twist[0] - x[0] * twist[1]], 0)
        x = jnp.einsum("crkb,cbdq->drkq", x, last, precision=PRECISE)
        x = jnp.stack([x[0] * turn[0] - x[1] * turn[1], x[0] * turn[1] + x[1] * turn[0]], 0)
        x = jnp.einsum("crkq,cqdb->drkb", x, last_back, precision=PRECISE)
        x = jnp.stack([x[0] * twist[0] - x[1] * twist[1], x[1] * twist[0] + x[0] * twist[1]], 0)
        return jnp.einsum("crkb,ckda->ardb", x, first_back, precision=PRECISE)

    raman = jnp.asarray(raman_matrix(block, halo), f32)
    all_profiles = lax.all_gather(modes, "mode", axis=1, tiled=True)
    all_modes = n_mode * own_modes

    def nonlinear(blocks):
        windows = jnp.stack([jnp.roll(blocks, halo - h, axis=0) for h in range(halo + 1)], 3)
        windows = lax.all_to_all(windows, BOTH, 0, 0, tiled=True)
        windows = windows.reshape(n_mode, n_tm * rows, 2, (halo + 1) * block)[:, :own_modes]
        windows = windows.reshape(all_modes, 2, (halo + 1) * block)
        grid = jnp.einsum("pg,pct->cgt", all_profiles, windows, precision=PRECISE)
        intensity = grid[0] * grid[0] + grid[1] * grid[1]
        delayed = jnp.dot(intensity, raman, precision=PRECISE)
        own = slice(halo * block, None)
        weight = (1.0 - RAMAN_SHARE) * intensity[:, own] + RAMAN_SHARE * delayed
        response = jnp.einsum("pg,cgt->pct", all_profiles, grid[:, :, own] * weight, precision=PRECISE)
        values = jnp.stack(
            [
                windows[:, 0, own] - KERR_GAIN * response[:, 1],
                windows[:, 1, own] + KERR_GAIN * response[:, 0],
            ],
            1,
        )
        values = jnp.pad(values.reshape(n_mode, own_modes, 2, block), ((0, 0), (0, spare), (0, 0), (0, 0)))
        return lax.all_to_all(values.reshape(n_dev, rows, 2, block), BOTH, 0, 0, tiled=True)

    entry = jnp.pad(field, ((0, spare), (0, 0), (0, 0))).reshape(n_tm, rows, 2, samples)
    entry = lax.all_to_all(entry, "tm", 0, 0, tiled=True)
    per_tm = samples // block
    blocks = entry.reshape(n_tm, rows, 2, per_tm, block).transpose(0, 3, 1, 2, 4).reshape(n_dev, rows, 2, block)
    blocks = disperse(blocks, half_turn)
    for number in range(ITERS):
        blocks = nonlinear(blocks)
        blocks = disperse(blocks, full_turn if number < ITERS - 1 else half_turn)
    leave = blocks.reshape(n_tm, per_tm, rows, 2, block).transpose(0, 2, 3, 1, 4).reshape(n_tm, rows, 2, samples)
    leave = lax.all_to_all(leave, "tm", 0, 0, tiled=True)
    return leave.reshape(n_tm * rows, 2, samples)[:own_modes]


def split_two(values):
    high = values.astype(jnp.bfloat16)
    return high, (values - high.astype(jnp.float32)).astype(jnp.bfloat16)


def np_split(values):
    high = values.astype(jnp.bfloat16)
    return high, (values - high.astype(np.float64)).astype(jnp.bfloat16)


def product(left, right):
    return jnp.dot(left, right, preferred_element_type=jnp.float32)


def cos_sin(angle):
    quarter = jnp.floor(angle * (2.0 / math.pi) + 0.5)
    rest = angle - quarter * 1.5703125
    rest = rest - quarter * 4.837512969970703e-4
    rest = rest - quarter * 7.549789948768648e-8
    square = rest * rest
    sine = rest + rest * square * (-1.6666654611e-1 + square * (8.3321608736e-3 - square * 1.9515295891e-4))
    cosine = 1.0 - 0.5 * square
    cosine = cosine + square * square * (
        4.166664568298827e-2 + square * (-1.388731625493765e-3 + square * 2.443315711809948e-5)
    )
    turn = quarter.astype(jnp.int32)
    odd = (turn & 1) == 1
    out_cos = jnp.where(odd, sine, cosine)
    out_sin = jnp.where(odd, cosine, sine)
    return (
        jnp.where(((turn + 1) & 2) == 2, -out_cos, out_cos),
        jnp.where((turn & 2) == 2, -out_sin, out_sin),
    )


def work_out_turns(total, rates_ref, half_ref, full_ref):
    rows = rates_ref.shape[0]
    _, count, block = half_ref.shape
    size = count // rows
    first, last = (lax.broadcasted_iota(jnp.int32, (size, block), d) for d in range(2))
    freq = first + size * last
    freq = jnp.where(freq < total // 2, freq, freq - total).astype(jnp.float32) * (2.0 / total)
    square = freq * freq
    scale = 1.0 / total
    for r in range(rows):
        phase = (
            rates_ref[r : r + 1, 0 : 1]
            + rates_ref[r : r + 1, 1 : 2] * freq
            + rates_ref[r : r + 1, 2 : 3] * square / 2.0
            + rates_ref[r : r + 1, 3 : 4] * (square * freq) / 6.0
        )
        cosine, sine = cos_sin(phase * 0.5)
        part = pl.ds(r * size, size)
        half_ref[0, part] = cosine * scale
        half_ref[1, part] = sine * scale
        full_ref[0, part] = (cosine * cosine - sine * sine) * scale
        full_ref[1, part] = (2.0 * scale) * cosine * sine


def profile_kernel(rows, *refs):
    pieces, taps_ref, (up_ref, down_ref, raman_ref) = refs[:-5], refs[-5], refs[-3:]
    window, double = raman_ref.shape
    block = double // 2
    taps = jnp.broadcast_to(taps_ref[0:1, :], (window, taps_ref.shape[1]))
    taps = pltpu.roll(taps, block, axis=1, stride=1, stride_axis=0)[:, :block]
    raman_ref[...] = jnp.concatenate(split_two(taps), axis=1)
    count = pieces[0].shape[0]
    n_dev = count // rows
    place, mode = (lax.broadcasted_iota(jnp.int32, (count, count), d) for d in range(2))
    order = (mode == (place % n_dev) * rows + place // n_dev).astype(jnp.float32).astype(jnp.bfloat16)
    start = 0
    for piece in pieces:
        width = piece.shape[1]
        wide, low = (product(order, part) for part in split_two(piece[...]))
        down_ref[:, start : start + width] = jnp.concatenate([wide, low], axis=0).astype(jnp.bfloat16)
        stack = jnp.concatenate([wide, low, wide, low], axis=0)
        up_ref[start : start + width, :] = stack.T.astype(jnp.bfloat16)
        start += width


def disperse_kernel(rows, total, load, store, x_ref, first_ref, last_ref, twist_ref, *refs):
    if total is not None:
        rates_ref, o_ref, turn_ref, full_ref = refs
        work_out_turns(total, rates_ref, turn_ref, full_ref)
    else:
        turn_ref, o_ref = refs
    n_dev, block = twist_ref.shape[1:]
    cos_high, sin_high, cos_low, sin_low = (last_ref[:, n * block : (n + 1) * block] for n in range(4))
    last_high = jnp.concatenate(
        [jnp.concatenate([cos_high, -sin_high], axis=1), jnp.concatenate([sin_high, cos_high], axis=1)], axis=0
    )
    last_low = jnp.concatenate(
        [jnp.concatenate([cos_low, -sin_low], axis=1), jnp.concatenate([sin_low, cos_low], axis=1)], axis=0
    )
    twist = [jnp.concatenate([twist_ref[c]] * rows, axis=1) for c in range(2)]

    def across(place, values):
        high, low = split_two(values)
        return product(first_ref[place], jnp.concatenate([high, high, low, low], axis=0))

    def twisted(values):
        re, im = values[:n_dev], values[n_dev:]
        return re * twist[0] + im * twist[1], im * twist[0] - re * twist[1]

    def along(re, im):
        high, low = split_two(jnp.concatenate([re, im], axis=1))
        both = product(jnp.concatenate([high, low], axis=0), last_high)
        size = high.shape[0]
        return both[:size] + both[size:] + product(high, last_low)

    def row_of(values):
        return jnp.concatenate([values[:, r * block : (r + 1) * block] for r in range(rows)], axis=0)

    def lane_of(values):
        return jnp.concatenate([values[r * n_dev : (r + 1) * n_dev] for r in range(rows)], axis=1)

    x = jnp.concatenate(
        [jnp.concatenate([load(x_ref, r, c) for r in range(rows)], axis=1) for c in range(2)], axis=0
    )
    re, im = twisted(across(0, x))
    z = along(row_of(re), row_of(im))
    z_re, z_im = z[:, :block], z[:, block:]
    turn_re, turn_im = turn_ref[0], turn_ref[1]
    z = along(z_re * turn_re - z_im * turn_im, -(z_re * turn_im + z_im * turn_re))
    re, im = twisted(jnp.concatenate([lane_of(z[:, :block]), lane_of(z[:, block:])], axis=0))
    x = across(1, jnp.concatenate([re, im], axis=0))
    for r in range(rows):
        lanes = slice(r * block, (r + 1) * block)
        store(o_ref, r, 0, x[:n_dev, lanes])
        store(o_ref, r, 1, -x[n_dev:, lanes])


def nonlinear_kernel(rows, halo, w_ref, up_ref, down_ref, raman_ref, o_ref):
    block = w_ref.shape[1]
    n_dev = w_ref.shape[0] // ((halo + 1) * rows * 2)
    n_modes = n_dev * rows
    chunk = (halo + 1) * rows * 2

    def part(h, c):
        return jnp.concatenate(
            [w_ref[pl.ds(h * 2 * rows + 2 * r + c, n_dev, stride=chunk), :] for r in range(rows)], axis=0
        )

    own, highs, lows = None, [], []
    for h in range(halo + 1):
        values = jnp.concatenate([part(h, 0), part(h, 1)], axis=1)
        high, low = split_two(values)
        if halo > 1 and h == 0:
            grid = product(up_ref[:, : 2 * n_modes], jnp.concatenate([high, high], axis=0))
        else:
            grid = product(up_ref[...], jnp.concatenate([high, high, low, low], axis=0))
        g_re, g_im = grid[:, :block], grid[:, block:]
        intensity = g_re * g_re + g_im * g_im
        high, low = split_two(intensity)
        highs.append(high)
        lows.append(low)
        if h == halo:
            own = (values, g_re, g_im, intensity)
    values, g_re, g_im, intensity = own
    taps = raman_ref[...]
    taps = jnp.concatenate(
        [taps, jnp.concatenate([taps[:, :block], jnp.zeros_like(taps[:, :block])], axis=1)], axis=0
    )
    both = product(jnp.concatenate(highs + lows, axis=1), taps)
    weight = (1.0 - RAMAN_SHARE) * intensity + (both[:, :block] + both[:, block:])
    drive = jnp.concatenate([g_re * weight, g_im * weight], axis=1)
    d_high, d_low = split_two(drive)
    both = product(down_ref[...], d_high)
    response = both[:n_modes] + both[n_modes:] + product(down_ref[:n_modes, :], d_low)
    out = [
        values[:, :block] - KERR_GAIN * response[:, block:],
        values[:, block:] + KERR_GAIN * response[:, :block],
    ]
    for c in range(2):
        for r in range(rows):
            o_ref[pl.ds(2 * r + c, n_dev, stride=2 * rows), :] = out[c][r * n_dev : (r + 1) * n_dev]


def tiled(field, modes, betas):
    n_mode, n_tm = lax.axis_size("mode"), lax.axis_size("tm")
    t_index = lax.axis_index("tm")
    own_modes, _, samples = field.shape
    n_dev = n_mode * n_tm
    total = samples * n_tm
    block = total // n_dev
    halo = -(-RAMAN_TAPS // block)
    rows = own_modes // n_tm
    per_tm = samples // block
    f32 = jnp.float32

    pieces = [modes]
    for shift in range(1, n_mode):
        pieces.append(lax.ppermute(modes, "mode", [(i, (i + shift) % n_mode) for i in range(n_mode)]))
    dev, pos = np.arange(n_dev), np.arange(block)
    cos_a, sin_a = exp_table(dev[:, None] * dev[None, :], n_dev)
    cos_t, sin_t = exp_table(dev[:, None] * pos[None, :], total)
    cos_b, sin_b = exp_table(pos[:, None] * pos[None, :], block)
    first = block_matrix(cos_a, sin_a).transpose(2, 3, 0, 1)
    (cos_high, cos_low), (sin_high, sin_low) = np_split(cos_b), np_split(sin_b)
    last = jnp.asarray(np.concatenate([cos_high, sin_high, cos_low, sin_low], axis=1))
    twist = jnp.asarray(np.stack([cos_t, sin_t]), f32)
    edge = np.arange(n_dev).reshape(n_tm, per_tm).T.reshape(-1)

    def flat(matrix):
        high, low = np_split(matrix.reshape(2 * n_dev, 2 * n_dev))
        return np.concatenate([high, low, high, low], axis=1)

    span = (halo + 1) * block
    lags = np.zeros((8, span + block))
    lags[:, block + 1 : block + 1 + RAMAN_TAPS] = RAMAN_SHARE * raman_taps()

    rates = lax.dynamic_slice_in_dim(betas, t_index * rows, rows, 0)

    def load_edge(ref, r, c):
        return jnp.concatenate(
            [
                ref[pl.ds(2 * (per_tm * r + q) + c, n_tm, stride=2 * per_tm * rows), :]
                for q in range(per_tm)
            ],
            axis=0,
        )

    def load_inner(ref, r, c):
        return ref[pl.ds(2 * r + c, n_dev, stride=2 * rows), :]

    def store_edge(ref, r, c, values):
        for q in range(per_tm):
            ref[:, r, c, q * block : (q + 1) * block] = values[q * n_tm : (q + 1) * n_tm]

    def store_inner(ref, r, c, values):
        for h in range(halo + 1):
            moved = pltpu.roll(values, halo - h, axis=0) if h < halo else values
            ref[pl.ds(2 * (h * rows + r) + c, n_dev, stride=2 * (halo + 1) * rows), :] = moved

    def disperse(values, turn, entering, leaving):
        shape = (n_tm, rows, 2, samples) if leaving else (n_dev * (halo + 1) * rows * 2, block)
        shape = jax.ShapeDtypeStruct(shape, f32)
        table = jax.ShapeDtypeStruct((2, rows * n_dev, block), f32)
        matrices = np.stack([flat(first[..., edge] if entering else first), flat(first[:, edge] if leaving else first)])
        return pl.pallas_call(
            functools.partial(
                disperse_kernel,
                rows,
                total if entering else None,
                load_edge if entering else load_inner,
                store_edge if leaving else store_inner,
            ),
            out_shape=(shape, table, table) if entering else shape,
                        name="disperse",
            compiler_params=PARAMS,
        )(values, jnp.asarray(matrices), last, twist, turn)

    def spread_profiles(windows):
        total_grid = modes.shape[1] * n_mode
        return pl.pallas_call(
            functools.partial(profile_kernel, rows),
            out_shape=(
                jax.ShapeDtypeStruct((total_grid, 4 * n_dev * rows), jnp.bfloat16),
                jax.ShapeDtypeStruct((2 * n_dev * rows, total_grid), jnp.bfloat16),
                jax.ShapeDtypeStruct((span, 2 * block), jnp.bfloat16),
            ),
            in_specs=[pl.BlockSpec(memory_space=pltpu.VMEM)] * (n_mode + 1) + [pl.BlockSpec(memory_space=pl.ANY)],
            name="profiles",
            compiler_params=PARAMS,
        )(*pieces, jnp.asarray(lags, f32), windows)

    def nonlinear(windows, up, down, raman):
        return pl.pallas_call(
            functools.partial(nonlinear_kernel, rows, halo),
            out_shape=jax.ShapeDtypeStruct((n_dev * rows * 2, block), f32),
            name="nonlinear",
            compiler_params=PARAMS,
        )(windows, up, down, raman)

    def exchange(values):
        shaped = values.reshape(n_dev, -1, 2, block)
        return lax.all_to_all(shaped, BOTH, 0, 0, tiled=True).reshape(-1, block)

    entry = field.reshape(own_modes, 2, per_tm, block)
    entry = with_layout_constraint(entry, Layout((0, 2, 1, 3)))
    entry = entry.transpose(0, 2, 1, 3).reshape(n_tm, rows * per_tm, 2, block)
    values = lax.all_to_all(entry, "tm", 0, 0, tiled=True).reshape(-1, block)
    values, half_turn, full_turn = disperse(values, rates, True, False)
    for number in range(ITERS):
        values = exchange(values)
        if number == 0:
            profiles = spread_profiles(values)
        values = nonlinear(values, *profiles)
        leaving = number == ITERS - 1
        values = disperse(exchange(values), half_turn if leaving else full_turn, False, leaving)
    return lax.all_to_all(values, "tm", 0, 0, tiled=True).reshape(field.shape)


def shards(field, modes, betas):
    n_mode, n_tm = lax.axis_size("mode"), lax.axis_size("tm")
    fits = (
        field.shape[2] % (128 * n_mode) == 0
        and field.shape[0] % n_tm == 0
        and n_tm % 8 == 0
        and modes.shape[1] % 128 == 0
    )
    if not fits:
        return general(field, modes, betas)
    return tiled(field, modes, betas)


def solution(mesh):
    return jax.shard_map(
        shards,
        mesh=mesh,
        in_specs=(P("mode", None, "tm"), P(None, "mode"), P("mode", None)),
        out_specs=P("mode", None, "tm"),
        check_vma=False,
    )
```

```python
import functools
import math

import jax
import jax.numpy as jnp
import numpy as np
from jax import lax
from jax.experimental import pallas as pl
from jax.experimental.layout import Layout, with_layout_constraint
from jax.experimental.pallas import tpu as pltpu
from jax.sharding import PartitionSpec as P


RAMAN_TAPS = 256
ITERS = 2
RAMAN_SHARE = 0.18
KERR_GAIN = 6.0
PRECISE = lax.Precision.HIGHEST
BOTH = ("mode", "tm")
PARAMS = pltpu.CompilerParams(vmem_limit_bytes=16 * 1024 * 1024)


def exp_table(product, length):
    angle = (product % length) * (2.0 * math.pi / length)
    return np.cos(angle), np.sin(angle)


def block_matrix(cosine, sine):
    return np.stack([np.stack([cosine, -sine], 1), np.stack([sine, cosine], 1)], 0)


def raman_taps():
    positions = np.arange(1, RAMAN_TAPS + 1)
    spacing = 256.0 / RAMAN_TAPS
    raw = np.exp(-positions * spacing / 32.0) * np.sin(positions * spacing / 12.2)
    return raw / raw.sum()


def raman_matrix(block, halo):
    taps = raman_taps()
    lag = np.arange(block)[None, :] + halo * block - np.arange((halo + 1) * block)[:, None]
    return np.where((lag >= 1) & (lag <= RAMAN_TAPS), taps[np.clip(lag, 1, RAMAN_TAPS) - 1], 0.0)


def general(field, modes, betas):
    n_mode, n_tm = lax.axis_size("mode"), lax.axis_size("tm")
    t_index = lax.axis_index("tm")
    own_modes, _, samples = field.shape
    n_dev = n_mode * n_tm
    total = samples * n_tm
    block = total // n_dev
    halo = -(-RAMAN_TAPS // block)
    rows = -(-own_modes // n_tm)
    spare = n_tm * rows - own_modes
    f32 = jnp.float32

    dev, pos = np.arange(n_dev), np.arange(block)
    cos_a, sin_a = exp_table(dev[:, None] * dev[None, :], n_dev)
    cos_t, sin_t = exp_table(dev[:, None] * pos[None, :], total)
    cos_b, sin_b = exp_table(pos[:, None] * pos[None, :], block)
    first = jnp.asarray(block_matrix(cos_a, sin_a), f32)
    first_back = jnp.asarray(block_matrix(cos_a, -sin_a) / total, f32)
    last = jnp.asarray(block_matrix(cos_b, sin_b), f32)
    last_back = jnp.asarray(block_matrix(cos_b, -sin_b), f32)
    twist = (jnp.asarray(cos_t, f32), jnp.asarray(sin_t, f32))

    frequency = dev[:, None] + n_dev * pos[None, :]
    norm_freq = jnp.asarray(np.where(frequency < total // 2, frequency, frequency - total) * (2.0 / total), f32)
    rates = lax.dynamic_slice_in_dim(jnp.pad(betas, ((0, spare), (0, 0))), t_index * rows, rows, 0)
    rates = rates[:, :, None, None]
    phase = (
        rates[:, 0]
        + rates[:, 1] * norm_freq
        + rates[:, 2] * (norm_freq * norm_freq) / 2.0
        + rates[:, 3] * (norm_freq * norm_freq * norm_freq) / 6.0
    )
    half_turn = (jnp.cos(phase * 0.5), jnp.sin(phase * 0.5))
    full_turn = (jnp.cos(phase), jnp.sin(phase))

    def disperse(blocks, turn):
        x = jnp.einsum("arcb,cadk->drkb", blocks, first, precision=PRECISE)
        x = jnp.stack([x[0] * twist[0] + x[1] * twist[1], x[1] * twist[0] - x[0] * twist[1]], 0)
        x = jnp.einsum("crkb,cbdq->drkq", x, last, precision=PRECISE)
        x = jnp.stack([x[0] * turn[0] - x[1] * turn[1], x[0] * turn[1] + x[1] * turn[0]], 0)
        x = jnp.einsum("crkq,cqdb->drkb", x, last_back, precision=PRECISE)
        x = jnp.stack([x[0] * twist[0] - x[1] * twist[1], x[1] * twist[0] + x[0] * twist[1]], 0)
        return jnp.einsum("crkb,ckda->ardb", x, first_back, precision=PRECISE)

    raman = jnp.asarray(raman_matrix(block, halo), f32)
    all_profiles = lax.all_gather(modes, "mode", axis=1, tiled=True)
    all_modes = n_mode * own_modes

    def nonlinear(blocks):
        windows = jnp.stack([jnp.roll(blocks, halo - h, axis=0) for h in range(halo + 1)], 3)
        windows = lax.all_to_all(windows, BOTH, 0, 0, tiled=True)
        windows = windows.reshape(n_mode, n_tm * rows, 2, (halo + 1) * block)[:, :own_modes]
        windows = windows.reshape(all_modes, 2, (halo + 1) * block)
        grid = jnp.einsum("pg,pct->cgt", all_profiles, windows, precision=PRECISE)
        intensity = grid[0] * grid[0] + grid[1] * grid[1]
        delayed = jnp.dot(intensity, raman, precision=PRECISE)
        own = slice(halo * block, None)
        weight = (1.0 - RAMAN_SHARE) * intensity[:, own] + RAMAN_SHARE * delayed
        response = jnp.einsum("pg,cgt->pct", all_profiles, grid[:, :, own] * weight, precision=PRECISE)
        values = jnp.stack(
            [
                windows[:, 0, own] - KERR_GAIN * response[:, 1],
                windows[:, 1, own] + KERR_GAIN * response[:, 0],
            ],
            1,
        )
        values = jnp.pad(values.reshape(n_mode, own_modes, 2, block), ((0, 0), (0, spare), (0, 0), (0, 0)))
        return lax.all_to_all(values.reshape(n_dev, rows, 2, block), BOTH, 0, 0, tiled=True)

    entry = jnp.pad(field, ((0, spare), (0, 0), (0, 0))).reshape(n_tm, rows, 2, samples)
    entry = lax.all_to_all(entry, "tm", 0, 0, tiled=True)
    per_tm = samples // block
    blocks = entry.reshape(n_tm, rows, 2, per_tm, block).transpose(0, 3, 1, 2, 4).reshape(n_dev, rows, 2, block)
    blocks = disperse(blocks, half_turn)
    for number in range(ITERS):
        blocks = nonlinear(blocks)
        blocks = disperse(blocks, full_turn if number < ITERS - 1 else half_turn)
    leave = blocks.reshape(n_tm, per_tm, rows, 2, block).transpose(0, 2, 3, 1, 4).reshape(n_tm, rows, 2, samples)
    leave = lax.all_to_all(leave, "tm", 0, 0, tiled=True)
    return leave.reshape(n_tm * rows, 2, samples)[:own_modes]


def split_two(values):
    high = values.astype(jnp.bfloat16)
    return high, (values - high.astype(jnp.float32)).astype(jnp.bfloat16)


def np_split(values):
    high = values.astype(jnp.bfloat16)
    return high, (values - high.astype(np.float64)).astype(jnp.bfloat16)


def product(left, right):
    return jnp.dot(left, right, preferred_element_type=jnp.float32)


def cos_sin(angle):
    quarter = jnp.floor(angle * (2.0 / math.pi) + 0.5)
    rest = angle - quarter * 1.5703125
    rest = rest - quarter * 4.837512969970703e-4
    rest = rest - quarter * 7.549789948768648e-8
    square = rest * rest
    sine = rest + rest * square * (-1.6666654611e-1 + square * (8.3321608736e-3 - square * 1.9515295891e-4))
    cosine = 1.0 - 0.5 * square
    cosine = cosine + square * square * (
        4.166664568298827e-2 + square * (-1.388731625493765e-3 + square * 2.443315711809948e-5)
    )
    turn = quarter.astype(jnp.int32)
    odd = (turn & 1) == 1
    out_cos = jnp.where(odd, sine, cosine)
    out_sin = jnp.where(odd, cosine, sine)
    return (
        jnp.where(((turn + 1) & 2) == 2, -out_cos, out_cos),
        jnp.where((turn & 2) == 2, -out_sin, out_sin),
    )


def work_out_turns(total, share, rates_ref, table_ref):
    rows = rates_ref.shape[0]
    _, count, block = table_ref.shape
    size = count // rows
    first, last = (lax.broadcasted_iota(jnp.int32, (size, block), d) for d in range(2))
    freq = first + size * last
    freq = jnp.where(freq < total // 2, freq, freq - total).astype(jnp.float32) * (2.0 / total)
    square = freq * freq
    scale = 1.0 / total
    for r in range(rows):
        phase = (
            rates_ref[r : r + 1, 0 : 1]
            + rates_ref[r : r + 1, 1 : 2] * freq
            + rates_ref[r : r + 1, 2 : 3] * square / 2.0
            + rates_ref[r : r + 1, 3 : 4] * (square * freq) / 6.0
        )
        cosine, sine = cos_sin(phase * share)
        part = pl.ds(r * size, size)
        table_ref[0, part] = cosine * scale
        table_ref[1, part] = sine * scale


def profile_kernel(rows, *refs):
    pieces, taps_ref, (up_ref, down_ref, raman_ref) = refs[:-5], refs[-5], refs[-3:]
    window, double = raman_ref.shape
    block = double // 2
    taps = jnp.broadcast_to(taps_ref[0:1, :], (window, taps_ref.shape[1]))
    taps = pltpu.roll(taps, block, axis=1, stride=1, stride_axis=0)[:, :block]
    raman_ref[...] = jnp.concatenate(split_two(taps), axis=1)
    count = pieces[0].shape[0]
    n_dev = count // rows
    place, mode = (lax.broadcasted_iota(jnp.int32, (count, count), d) for d in range(2))
    order = (mode == (place % n_dev) * rows + place // n_dev).astype(jnp.float32).astype(jnp.bfloat16)
    start = 0
    for piece in pieces:
        width = piece.shape[1]
        wide, low = (product(order, part) for part in split_two(piece[...]))
        down_ref[:, start : start + width] = jnp.concatenate([wide, low], axis=0).astype(jnp.bfloat16)
        stack = jnp.concatenate([wide, low, wide, low], axis=0)
        up_ref[start : start + width, :] = stack.T.astype(jnp.bfloat16)
        start += width


def disperse_kernel(rows, total, share, load, store, x_ref, first_ref, final_ref, last_ref, twist_ref, *refs):
    if total is None:
        turn_ref, o_ref = refs
    else:
        o_ref, turn_ref = refs[-2:]
        work_out_turns(total, share, refs[0], turn_ref)
    n_dev, block = twist_ref.shape[1:]
    cos_high, sin_high, cos_low, sin_low = (last_ref[:, n * block : (n + 1) * block] for n in range(4))
    last_high = jnp.concatenate(
        [jnp.concatenate([cos_high, -sin_high], axis=1), jnp.concatenate([sin_high, cos_high], axis=1)], axis=0
    )
    last_low = jnp.concatenate(
        [jnp.concatenate([cos_low, -sin_low], axis=1), jnp.concatenate([sin_low, cos_low], axis=1)], axis=0
    )
    twist = [jnp.concatenate([twist_ref[c]] * rows, axis=1) for c in range(2)]

    def across(matrix_ref, values):
        high, low = split_two(values)
        return product(matrix_ref[...], jnp.concatenate([high, high, low, low], axis=0))

    def twisted(values):
        re, im = values[:n_dev], values[n_dev:]
        return re * twist[0] + im * twist[1], im * twist[0] - re * twist[1]

    def along(re, im):
        high, low = split_two(jnp.concatenate([re, im], axis=1))
        both = product(jnp.concatenate([high, low], axis=0), last_high)
        size = high.shape[0]
        return both[:size] + both[size:] + product(high, last_low)

    def row_of(values):
        return jnp.concatenate([values[:, r * block : (r + 1) * block] for r in range(rows)], axis=0)

    def lane_of(values):
        return jnp.concatenate([values[r * n_dev : (r + 1) * n_dev] for r in range(rows)], axis=1)

    x = jnp.concatenate(
        [jnp.concatenate([load(x_ref, r, c) for r in range(rows)], axis=1) for c in range(2)], axis=0
    )
    re, im = twisted(across(first_ref, x))
    z = along(row_of(re), row_of(im))
    z_re, z_im = z[:, :block], z[:, block:]
    turn_re, turn_im = turn_ref[0], turn_ref[1]
    z = along(z_re * turn_re - z_im * turn_im, -(z_re * turn_im + z_im * turn_re))
    re, im = twisted(jnp.concatenate([lane_of(z[:, :block]), lane_of(z[:, block:])], axis=0))
    x = across(final_ref, jnp.concatenate([re, im], axis=0))
    for r in range(rows):
        lanes = slice(r * block, (r + 1) * block)
        store(o_ref, r, 0, x[: x.shape[0] // 2, lanes])
        store(o_ref, r, 1, -x[x.shape[0] // 2 :, lanes])


def nonlinear_kernel(rows, halo, load, store, w_ref, up_ref, down_ref, raman_ref, o_ref):
    block = w_ref.shape[1]
    n_modes = up_ref.shape[1] // 4
    count = n_modes // rows

    def part(h, c):
        return jnp.concatenate([load(w_ref, h, r, c) for r in range(rows)], axis=0)

    own, highs, lows = None, [], []
    for h in range(halo + 1):
        values = jnp.concatenate([part(h, 0), part(h, 1)], axis=1)
        high, low = split_two(values)
        if halo > 1 and h == 0:
            grid = product(up_ref[:, : 2 * n_modes], jnp.concatenate([high, high], axis=0))
        else:
            grid = product(up_ref[...], jnp.concatenate([high, high, low, low], axis=0))
        g_re, g_im = grid[:, :block], grid[:, block:]
        intensity = g_re * g_re + g_im * g_im
        high, low = split_two(intensity)
        highs.append(high)
        lows.append(low)
        if h == halo:
            own = (values, g_re, g_im, intensity)
    values, g_re, g_im, intensity = own
    taps = raman_ref[...]
    taps = jnp.concatenate(
        [taps, jnp.concatenate([taps[:, :block], jnp.zeros_like(taps[:, :block])], axis=1)], axis=0
    )
    both = product(jnp.concatenate(highs + lows, axis=1), taps)
    weight = (1.0 - RAMAN_SHARE) * intensity + (both[:, :block] + both[:, block:])
    drive = jnp.concatenate([g_re * weight, g_im * weight], axis=1)
    d_high, d_low = split_two(drive)
    both = product(down_ref[...], d_high)
    response = both[:n_modes] + both[n_modes:] + product(down_ref[:n_modes, :], d_low)
    out = [
        values[:, :block] - KERR_GAIN * response[:, block:],
        values[:, block:] + KERR_GAIN * response[:, :block],
    ]
    for c in range(2):
        for r in range(rows):
            store(o_ref, r, c, out[c][r * count : (r + 1) * count])


def tiled(field, modes, betas):
    n_mode, n_tm = lax.axis_size("mode"), lax.axis_size("tm")
    t_index = lax.axis_index("tm")
    own_modes, _, samples = field.shape
    n_dev = n_mode * n_tm
    total = samples * n_tm
    block = total // n_dev
    halo = -(-RAMAN_TAPS // block)
    rows = own_modes // n_tm
    per_tm = samples // block
    f32 = jnp.float32

    quarter = n_tm // 2
    n_pair = n_mode * quarter
    wide = 2 * rows
    halves = [[m * n_tm + h * quarter + q for m in range(n_mode) for q in range(quarter)] for h in range(2)]
    both_halves = [halves[0] + halves[1]]
    half = t_index // quarter

    pieces = [modes]
    for shift in range(1, n_mode):
        pieces.append(lax.ppermute(modes, "mode", [(i, (i + shift) % n_mode) for i in range(n_mode)]))
    dev, pos = np.arange(n_dev), np.arange(block)
    cos_a, sin_a = exp_table(dev[:, None] * dev[None, :], n_dev)
    cos_t, sin_t = exp_table(dev[:, None] * pos[None, :], total)
    cos_b, sin_b = exp_table(pos[:, None] * pos[None, :], block)
    first = block_matrix(cos_a, sin_a).transpose(2, 3, 0, 1)
    (cos_high, cos_low), (sin_high, sin_low) = np_split(cos_b), np_split(sin_b)
    last = jnp.asarray(np.concatenate([cos_high, sin_high, cos_low, sin_low], axis=1))
    twist = jnp.asarray(np.stack([cos_t, sin_t]), f32)
    edge = np.arange(n_dev).reshape(n_tm, per_tm).T.reshape(-1)

    def flat(matrix):
        high, low = np_split(matrix.reshape(-1, 2 * n_dev))
        return np.concatenate([high, low, high, low], axis=1)

    span = (halo + 1) * block
    lags = np.zeros((8, span + block))
    lags[:, block + 1 : block + 1 + RAMAN_TAPS] = RAMAN_SHARE * raman_taps()

    rates = lax.dynamic_slice_in_dim(betas, t_index * rows, rows, 0)
    rates_wide = lax.dynamic_slice_in_dim(betas, (t_index % quarter) * wide, wide, 0)
    windows_of = [[(a - halo + h) % n_dev for h in range(halo + 1) for a in devices] for devices in halves]
    final_wide = jnp.asarray(np.stack([flat(first[:, blocks]) for blocks in windows_of]))
    final_wide = lax.dynamic_index_in_dim(final_wide, half, 0, keepdims=False)

    def load_edge(ref, r, c):
        return jnp.concatenate(
            [
                ref[pl.ds(2 * (per_tm * r + q) + c, n_tm, stride=2 * per_tm * rows), :]
                for q in range(per_tm)
            ],
            axis=0,
        )

    def load_inner(ref, r, c):
        return ref[pl.ds(2 * r + c, n_dev, stride=2 * rows), :]

    def store_edge(ref, r, c, values):
        for q in range(per_tm):
            ref[:, r, c, q * block : (q + 1) * block] = values[q * n_tm : (q + 1) * n_tm]

    def store_inner(ref, r, c, values):
        for h in range(halo + 1):
            moved = pltpu.roll(values, halo - h, axis=0) if h < halo else values
            ref[pl.ds(2 * (h * rows + r) + c, n_dev, stride=2 * (halo + 1) * rows), :] = moved

    def load_wide(ref, r, c):
        return ref[pl.ds(2 * r + c, n_dev, stride=2 * wide), :]

    def store_wide(ref, r, c, values):
        for h in range(halo + 1):
            ref[pl.ds(2 * (h * wide + r) + c, n_pair, stride=2 * (halo + 1) * wide), :] = values[
                h * n_pair : (h + 1) * n_pair
            ]

    def call_disperse(kernel, shape, *operands, **options):
        return pl.pallas_call(kernel, out_shape=shape, compiler_params=PARAMS, **options)(*operands)

    def table_of(count):
        return (2, count * n_dev, block)

    def enter(values):
        kernel = functools.partial(disperse_kernel, rows, total, 0.5, load_edge, store_inner)
        shapes = ((n_dev * (halo + 1) * rows * 2, block), table_of(rows))
        matrices = (jnp.asarray(flat(first[..., edge])), jnp.asarray(flat(first)))
        return call_disperse(
            kernel,
            tuple(jax.ShapeDtypeStruct(shape, f32) for shape in shapes),
            *(values, *matrices, last, twist, rates, rates_wide, final_wide),
        )

    def go_on(values):
        kernel = functools.partial(disperse_kernel, wide, total, 1.0, load_wide, store_wide)
        shape = jax.ShapeDtypeStruct((n_pair * (halo + 1) * wide * 2, block), f32)
        return call_disperse(
            kernel,
            shape,
            *(values, jnp.asarray(flat(first[..., both_halves[0]])), final_wide, last, twist, rates_wide),
            scratch_shapes=[pltpu.VMEM(table_of(wide), f32)],
        )

    def leave(values, turn):
        kernel = functools.partial(disperse_kernel, rows, None, None, load_inner, store_edge)
        shape = jax.ShapeDtypeStruct((n_tm, rows, 2, samples), f32)
        matrices = (jnp.asarray(flat(first)), jnp.asarray(flat(first[:, edge])))
        return call_disperse(kernel, shape, values, *matrices, last, twist, turn)

    def spread_profiles(windows):
        total_grid = modes.shape[1] * n_mode
        return pl.pallas_call(
            functools.partial(profile_kernel, wide),
            out_shape=(
                jax.ShapeDtypeStruct((total_grid, 4 * n_dev * rows), jnp.bfloat16),
                jax.ShapeDtypeStruct((2 * n_dev * rows, total_grid), jnp.bfloat16),
                jax.ShapeDtypeStruct((span, 2 * block), jnp.bfloat16),
            ),
            in_specs=[pl.BlockSpec(memory_space=pltpu.VMEM)] * (n_mode + 1) + [pl.BlockSpec(memory_space=pl.ANY)],
            name="profiles",
            compiler_params=PARAMS,
        )(*pieces, jnp.asarray(lags, f32), windows)

    def load_spread(ref, h, r, c):
        start = (r // rows) * 2 * (halo + 1) * rows + 2 * (h * rows + r % rows) + c
        return ref[pl.ds(start, n_pair, stride=4 * (halo + 1) * rows), :]

    def load_half(ref, h, r, c):
        return ref[pl.ds(2 * (h * wide + r) + c, n_pair, stride=2 * (halo + 1) * wide), :]

    def store_halves(ref, r, c, values):
        for h in range(2):
            ref[pl.ds(h * n_pair * 2 * wide + 2 * r + c, n_pair, stride=2 * wide), :] = values

    def store_last(ref, r, c, values):
        ref[pl.ds((r // rows) * 2 * rows + 2 * (r % rows) + c, n_pair, stride=4 * rows), :] = values

    def nonlinear(number, windows, up, down, raman):
        is_last = number == ITERS - 1
        height = n_dev * (rows if is_last else wide) * 2
        return pl.pallas_call(
            functools.partial(
                nonlinear_kernel,
                wide,
                halo,
                load_half if number else load_spread,
                store_last if is_last else store_halves,
            ),
            out_shape=jax.ShapeDtypeStruct((height, block), f32),
            name="nonlinear",
            compiler_params=PARAMS,
        )(windows, up, down, raman)

    def exchange(values, groups=None):
        count = len(groups[0]) if groups else n_dev
        shaped = values.reshape(count, -1, 2, block)
        return lax.all_to_all(shaped, BOTH, 0, 0, tiled=True, axis_index_groups=groups).reshape(-1, block)

    entry = field.reshape(own_modes, 2, per_tm, block)
    entry = with_layout_constraint(entry, Layout((0, 2, 1, 3)))
    entry = entry.transpose(0, 2, 1, 3).reshape(n_tm, rows * per_tm, 2, block)
    values = lax.all_to_all(entry, "tm", 0, 0, tiled=True).reshape(-1, block)
    values, half_turn = enter(values)
    values = exchange(values)
    profiles = spread_profiles(values)
    for number in range(ITERS):
        values = nonlinear(number, values, *profiles)
        if number < ITERS - 1:
            values = go_on(exchange(values, both_halves))
            values = exchange(values, halves)
    values = leave(exchange(values), half_turn)
    return lax.all_to_all(values, "tm", 0, 0, tiled=True).reshape(field.shape)


def shards(field, modes, betas):
    n_mode, n_tm = lax.axis_size("mode"), lax.axis_size("tm")
    fits = (
        field.shape[2] % (128 * n_mode) == 0
        and field.shape[0] % n_tm == 0
        and n_tm % 8 == 0
        and modes.shape[1] % 128 == 0
    )
    if not fits:
        return general(field, modes, betas)
    return tiled(field, modes, betas)


def solution(mesh):
    return jax.shard_map(
        shards,
        mesh=mesh,
        in_specs=(P("mode", None, "tm"), P(None, "mode"), P("mode", None)),
        out_specs=P("mode", None, "tm"),
        check_vma=False,
    )
```

```python
import functools
import math

import jax
import jax.numpy as jnp
import numpy as np
from jax import lax
from jax.experimental import pallas as pl
from jax.experimental.layout import Layout, with_layout_constraint
from jax.experimental.pallas import tpu as pltpu
from jax.sharding import PartitionSpec as P


RAMAN_TAPS = 256
ITERS = 2
RAMAN_SHARE = 0.18
KERR_GAIN = 6.0
PRECISE = lax.Precision.HIGHEST
BOTH = ("mode", "tm")
PARAMS = pltpu.CompilerParams(vmem_limit_bytes=16 * 1024 * 1024)


def exp_table(product, length):
    angle = (product % length) * (2.0 * math.pi / length)
    return np.cos(angle), np.sin(angle)


def block_matrix(cosine, sine):
    return np.stack([np.stack([cosine, -sine], 1), np.stack([sine, cosine], 1)], 0)


def raman_taps():
    positions = np.arange(1, RAMAN_TAPS + 1)
    spacing = 256.0 / RAMAN_TAPS
    raw = np.exp(-positions * spacing / 32.0) * np.sin(positions * spacing / 12.2)
    return raw / raw.sum()


def raman_matrix(block, halo):
    taps = raman_taps()
    lag = np.arange(block)[None, :] + halo * block - np.arange((halo + 1) * block)[:, None]
    return np.where((lag >= 1) & (lag <= RAMAN_TAPS), taps[np.clip(lag, 1, RAMAN_TAPS) - 1], 0.0)


def general(field, modes, betas):
    n_mode, n_tm = lax.axis_size("mode"), lax.axis_size("tm")
    t_index = lax.axis_index("tm")
    own_modes, _, samples = field.shape
    n_dev = n_mode * n_tm
    total = samples * n_tm
    block = total // n_dev
    halo = -(-RAMAN_TAPS // block)
    rows = -(-own_modes // n_tm)
    spare = n_tm * rows - own_modes
    f32 = jnp.float32

    dev, pos = np.arange(n_dev), np.arange(block)
    cos_a, sin_a = exp_table(dev[:, None] * dev[None, :], n_dev)
    cos_t, sin_t = exp_table(dev[:, None] * pos[None, :], total)
    cos_b, sin_b = exp_table(pos[:, None] * pos[None, :], block)
    first = jnp.asarray(block_matrix(cos_a, sin_a), f32)
    first_back = jnp.asarray(block_matrix(cos_a, -sin_a) / total, f32)
    last = jnp.asarray(block_matrix(cos_b, sin_b), f32)
    last_back = jnp.asarray(block_matrix(cos_b, -sin_b), f32)
    twist = (jnp.asarray(cos_t, f32), jnp.asarray(sin_t, f32))

    frequency = dev[:, None] + n_dev * pos[None, :]
    norm_freq = jnp.asarray(np.where(frequency < total // 2, frequency, frequency - total) * (2.0 / total), f32)
    rates = lax.dynamic_slice_in_dim(jnp.pad(betas, ((0, spare), (0, 0))), t_index * rows, rows, 0)
    rates = rates[:, :, None, None]
    phase = (
        rates[:, 0]
        + rates[:, 1] * norm_freq
        + rates[:, 2] * (norm_freq * norm_freq) / 2.0
        + rates[:, 3] * (norm_freq * norm_freq * norm_freq) / 6.0
    )
    half_turn = (jnp.cos(phase * 0.5), jnp.sin(phase * 0.5))
    full_turn = (jnp.cos(phase), jnp.sin(phase))

    def disperse(blocks, turn):
        x = jnp.einsum("arcb,cadk->drkb", blocks, first, precision=PRECISE)
        x = jnp.stack([x[0] * twist[0] + x[1] * twist[1], x[1] * twist[0] - x[0] * twist[1]], 0)
        x = jnp.einsum("crkb,cbdq->drkq", x, last, precision=PRECISE)
        x = jnp.stack([x[0] * turn[0] - x[1] * turn[1], x[0] * turn[1] + x[1] * turn[0]], 0)
        x = jnp.einsum("crkq,cqdb->drkb", x, last_back, precision=PRECISE)
        x = jnp.stack([x[0] * twist[0] - x[1] * twist[1], x[1] * twist[0] + x[0] * twist[1]], 0)
        return jnp.einsum("crkb,ckda->ardb", x, first_back, precision=PRECISE)

    raman = jnp.asarray(raman_matrix(block, halo), f32)
    all_profiles = lax.all_gather(modes, "mode", axis=1, tiled=True)
    all_modes = n_mode * own_modes

    def nonlinear(blocks):
        windows = jnp.stack([jnp.roll(blocks, halo - h, axis=0) for h in range(halo + 1)], 3)
        windows = lax.all_to_all(windows, BOTH, 0, 0, tiled=True)
        windows = windows.reshape(n_mode, n_tm * rows, 2, (halo + 1) * block)[:, :own_modes]
        windows = windows.reshape(all_modes, 2, (halo + 1) * block)
        grid = jnp.einsum("pg,pct->cgt", all_profiles, windows, precision=PRECISE)
        intensity = grid[0] * grid[0] + grid[1] * grid[1]
        delayed = jnp.dot(intensity, raman, precision=PRECISE)
        own = slice(halo * block, None)
        weight = (1.0 - RAMAN_SHARE) * intensity[:, own] + RAMAN_SHARE * delayed
        response = jnp.einsum("pg,cgt->pct", all_profiles, grid[:, :, own] * weight, precision=PRECISE)
        values = jnp.stack(
            [
                windows[:, 0, own] - KERR_GAIN * response[:, 1],
                windows[:, 1, own] + KERR_GAIN * response[:, 0],
            ],
            1,
        )
        values = jnp.pad(values.reshape(n_mode, own_modes, 2, block), ((0, 0), (0, spare), (0, 0), (0, 0)))
        return lax.all_to_all(values.reshape(n_dev, rows, 2, block), BOTH, 0, 0, tiled=True)

    entry = jnp.pad(field, ((0, spare), (0, 0), (0, 0))).reshape(n_tm, rows, 2, samples)
    entry = lax.all_to_all(entry, "tm", 0, 0, tiled=True)
    per_tm = samples // block
    blocks = entry.reshape(n_tm, rows, 2, per_tm, block).transpose(0, 3, 1, 2, 4).reshape(n_dev, rows, 2, block)
    blocks = disperse(blocks, half_turn)
    for number in range(ITERS):
        blocks = nonlinear(blocks)
        blocks = disperse(blocks, full_turn if number < ITERS - 1 else half_turn)
    leave = blocks.reshape(n_tm, per_tm, rows, 2, block).transpose(0, 2, 3, 1, 4).reshape(n_tm, rows, 2, samples)
    leave = lax.all_to_all(leave, "tm", 0, 0, tiled=True)
    return leave.reshape(n_tm * rows, 2, samples)[:own_modes]


def split_two(values):
    high = values.astype(jnp.bfloat16)
    return high, (values - high.astype(jnp.float32)).astype(jnp.bfloat16)


def np_split(values):
    high = values.astype(jnp.bfloat16)
    return high, (values - high.astype(np.float64)).astype(jnp.bfloat16)


def product(left, right):
    return jnp.dot(left, right, preferred_element_type=jnp.float32)


def cos_sin(angle):
    quarter = jnp.floor(angle * (2.0 / math.pi) + 0.5)
    rest = angle - quarter * 1.5703125
    rest = rest - quarter * 4.837512969970703e-4
    rest = rest - quarter * 7.549789948768648e-8
    square = rest * rest
    sine = rest + rest * square * (-1.6666654611e-1 + square * (8.3321608736e-3 - square * 1.9515295891e-4))
    cosine = 1.0 - 0.5 * square
    cosine = cosine + square * square * (
        4.166664568298827e-2 + square * (-1.388731625493765e-3 + square * 2.443315711809948e-5)
    )
    turn = quarter.astype(jnp.int32)
    odd = (turn & 1) == 1
    out_cos = jnp.where(odd, sine, cosine)
    out_sin = jnp.where(odd, cosine, sine)
    return (
        jnp.where(((turn + 1) & 2) == 2, -out_cos, out_cos),
        jnp.where((turn & 2) == 2, -out_sin, out_sin),
    )


def work_out_turns(total, share, rows, start, betas_ref, table_ref):
    _, count, block = table_ref.shape
    size = count // rows
    first, last = (lax.broadcasted_iota(jnp.int32, (size, block), d) for d in range(2))
    freq = first + size * last
    freq = jnp.where(freq < total // 2, freq, freq - total).astype(jnp.float32) * (2.0 / total)
    square = freq * freq
    scale = 1.0 / total
    for r in range(rows):
        rates = betas_ref[pl.ds(start + r, 1), :]
        phase = (
            rates[:, 0 : 1]
            + rates[:, 1 : 2] * freq
            + rates[:, 2 : 3] * square / 2.0
            + rates[:, 3 : 4] * (square * freq) / 6.0
        )
        cosine, sine = cos_sin(phase * share)
        part = pl.ds(r * size, size)
        table_ref[0, part] = cosine * scale
        table_ref[1, part] = sine * scale


def make_profiles(rows, pieces, taps_ref, up_ref, down_ref, raman_ref):
    window, double = raman_ref.shape
    block = double // 2
    taps = jnp.broadcast_to(taps_ref[0:1, :], (window, taps_ref.shape[1]))
    taps = pltpu.roll(taps, block, axis=1, stride=1, stride_axis=0)[:, :block]
    raman_ref[...] = jnp.concatenate(split_two(taps), axis=1)
    count = pieces[0].shape[0]
    n_dev = count // rows
    place, mode = (lax.broadcasted_iota(jnp.int32, (count, count), d) for d in range(2))
    order = (mode == (place % n_dev) * rows + place // n_dev).astype(jnp.float32).astype(jnp.bfloat16)
    start = 0
    for piece in pieces:
        width = piece.shape[1]
        wide, low = (product(order, part) for part in split_two(piece[...]))
        down_ref[:, start : start + width] = jnp.concatenate([wide, low], axis=0).astype(jnp.bfloat16)
        stack = jnp.concatenate([wide, low, wide], axis=0)
        up_ref[start : start + width, :] = stack.T.astype(jnp.bfloat16)
        start += width


def disperse_kernel(rows, total, share, joined, load, store, x_ref, *refs):
    count = 1 if joined else 2
    matrices, last_ref, refs = refs[:count], refs[count], refs[count + 1 :]
    n_dev, block = matrices[0].shape[1] // 2, last_ref.shape[0]
    if total is None:
        turn_ref, o_ref = refs
    else:
        betas_ref, o_ref, turn_ref = refs
        place = lax.axis_index("tm")
        holders = betas_ref.shape[0] // rows
        work_out_turns(total, share, rows, place % holders * rows, betas_ref, turn_ref)
        place = place // holders
    cos_high, sin_high, cos_low, sin_low = (last_ref[:, n * block : (n + 1) * block] for n in range(4))
    last_high = jnp.concatenate(
        [jnp.concatenate([cos_high, -sin_high], axis=1), jnp.concatenate([sin_high, cos_high], axis=1)], axis=0
    )
    last_low = jnp.concatenate(
        [jnp.concatenate([cos_low, -sin_low], axis=1), jnp.concatenate([sin_low, cos_low], axis=1)], axis=0
    )
    place_of, time_of = (lax.broadcasted_iota(jnp.int32, (n_dev, block), d) for d in range(2))
    twist = cos_sin((place_of * time_of).astype(jnp.float32) * (2.0 * math.pi / (n_dev * block)))
    twist = [jnp.concatenate([part] * rows, axis=1) for part in twist]

    def across(matrix, values):
        high, low = split_two(values)
        matrix = jnp.concatenate([matrix, matrix], axis=1)
        return product(matrix, jnp.concatenate([high, high, low, low], axis=0))

    def twisted(values):
        re, im = values[:n_dev], values[n_dev:]
        return re * twist[0] + im * twist[1], im * twist[0] - re * twist[1]

    def along(re, im):
        high, low = split_two(jnp.concatenate([re, im], axis=1))
        both = product(jnp.concatenate([high, low], axis=0), last_high)
        size = high.shape[0]
        return both[:size] + both[size:] + product(high, last_low)

    def row_of(values):
        return jnp.concatenate([values[:, r * block : (r + 1) * block] for r in range(rows)], axis=0)

    def lane_of(values):
        return jnp.concatenate([values[r * n_dev : (r + 1) * n_dev] for r in range(rows)], axis=1)

    x = jnp.concatenate(
        [jnp.concatenate([load(x_ref, r, c) for r in range(rows)], axis=1) for c in range(2)], axis=0
    )
    re, im = twisted(across(matrices[0][0], x))
    z = along(row_of(re), row_of(im))
    z_re, z_im = z[:, :block], z[:, block:]
    turn_re, turn_im = turn_ref[0], turn_ref[1]
    z = along(z_re * turn_re - z_im * turn_im, -(z_re * turn_im + z_im * turn_re))
    re, im = twisted(jnp.concatenate([lane_of(z[:, :block]), lane_of(z[:, block:])], axis=0))
    x = across(matrices[0][1] if joined else matrices[1][place], jnp.concatenate([re, im], axis=0))
    for r in range(rows):
        lanes = slice(r * block, (r + 1) * block)
        store(o_ref, r, 0, x[: x.shape[0] // 2, lanes])
        store(o_ref, r, 1, -x[x.shape[0] // 2 :, lanes])


def nonlinear_kernel(rows, halo, load, store, pieces, w_ref, *refs):
    if pieces:
        o_ref, up_ref, down_ref, raman_ref = refs[pieces + 1 :]
        make_profiles(rows, refs[:pieces], refs[pieces], up_ref, down_ref, raman_ref)
    else:
        up_ref, down_ref, raman_ref, o_ref = refs
    block = w_ref.shape[1]
    n_modes = up_ref.shape[1] // 3
    count = n_modes // rows

    def part(h, c):
        return jnp.concatenate([load(w_ref, h, r, c) for r in range(rows)], axis=0)

    own, highs, lows = None, [], []
    for h in range(halo + 1):
        values = jnp.concatenate([part(h, 0), part(h, 1)], axis=1)
        high, low = split_two(values)
        if halo > 1 and h == 0:
            grid = product(up_ref[:, : 2 * n_modes], jnp.concatenate([high, high], axis=0))
        else:
            grid = product(up_ref[...], jnp.concatenate([high, high, low], axis=0))
        g_re, g_im = grid[:, :block], grid[:, block:]
        intensity = g_re * g_re + g_im * g_im
        high, low = split_two(intensity)
        highs.append(high)
        lows.append(low)
        if h == halo:
            own = (values, g_re, g_im, intensity)
    values, g_re, g_im, intensity = own
    taps = raman_ref[...]
    taps = jnp.concatenate(
        [taps, jnp.concatenate([taps[:, :block], jnp.zeros_like(taps[:, :block])], axis=1)], axis=0
    )
    both = product(jnp.concatenate(highs + lows, axis=1), taps)
    weight = (1.0 - RAMAN_SHARE) * intensity + (both[:, :block] + both[:, block:])
    drive = jnp.concatenate([g_re * weight, g_im * weight], axis=1)
    d_high, d_low = split_two(drive)
    both = product(down_ref[...], d_high)
    response = both[:n_modes] + both[n_modes:] + product(down_ref[:n_modes, :], d_low)
    out = [
        values[:, :block] - KERR_GAIN * response[:, block:],
        values[:, block:] + KERR_GAIN * response[:, :block],
    ]
    for c in range(2):
        for r in range(rows):
            store(o_ref, r, c, out[c][r * count : (r + 1) * count])


def tiled(field, modes, betas):
    n_mode, n_tm = lax.axis_size("mode"), lax.axis_size("tm")
    own_modes, _, samples = field.shape
    n_dev = n_mode * n_tm
    total = samples * n_tm
    block = total // n_dev
    halo = -(-RAMAN_TAPS // block)
    rows = own_modes // n_tm
    per_tm = samples // block
    f32 = jnp.float32

    quarter = n_tm // 2
    n_pair = n_mode * quarter
    wide = 2 * rows
    halves = [[m * n_tm + h * quarter + q for m in range(n_mode) for q in range(quarter)] for h in range(2)]
    both_halves = [halves[0] + halves[1]]

    pieces = [modes]
    for shift in range(1, n_mode):
        pieces.append(lax.ppermute(modes, "mode", [(i, (i + shift) % n_mode) for i in range(n_mode)]))
    dev, pos = np.arange(n_dev), np.arange(block)
    cos_a, sin_a = exp_table(dev[:, None] * dev[None, :], n_dev)
    cos_b, sin_b = exp_table(pos[:, None] * pos[None, :], block)
    first = block_matrix(cos_a, sin_a).transpose(2, 3, 0, 1)
    (cos_high, cos_low), (sin_high, sin_low) = np_split(cos_b), np_split(sin_b)
    last = jnp.asarray(np.concatenate([cos_high, sin_high, cos_low, sin_low], axis=1))
    edge = np.arange(n_dev).reshape(n_tm, per_tm).T.reshape(-1)

    def flat(matrix):
        high, low = np_split(matrix.reshape(-1, 2 * n_dev))
        return np.concatenate([high, low], axis=1)

    span = (halo + 1) * block
    lags = np.zeros((8, span + block))
    lags[:, block + 1 : block + 1 + RAMAN_TAPS] = RAMAN_SHARE * raman_taps()

    windows_of = [[(a - halo + h) % n_dev for h in range(halo + 1) for a in devices] for devices in halves]
    final_wide = jnp.asarray(np.stack([flat(first[:, blocks]) for blocks in windows_of]))

    def load_edge(ref, r, c):
        return jnp.concatenate(
            [
                ref[pl.ds(2 * (per_tm * r + q) + c, n_tm, stride=2 * per_tm * rows), :]
                for q in range(per_tm)
            ],
            axis=0,
        )

    def load_inner(ref, r, c):
        return ref[pl.ds(2 * r + c, n_dev, stride=2 * rows), :]

    def store_edge(ref, r, c, values):
        for q in range(per_tm):
            ref[:, r, c, q * block : (q + 1) * block] = values[q * n_tm : (q + 1) * n_tm]

    def store_inner(ref, r, c, values):
        for h in range(halo + 1):
            moved = pltpu.roll(values, halo - h, axis=0) if h < halo else values
            ref[pl.ds(2 * (h * rows + r) + c, n_dev, stride=2 * (halo + 1) * rows), :] = moved

    def load_wide(ref, r, c):
        return ref[pl.ds(2 * r + c, n_dev, stride=2 * wide), :]

    def store_wide(ref, r, c, values):
        for h in range(halo + 1):
            ref[pl.ds(2 * (h * wide + r) + c, n_pair, stride=2 * (halo + 1) * wide), :] = values[
                h * n_pair : (h + 1) * n_pair
            ]

    def call_disperse(kernel, shape, *operands, **options):
        return pl.pallas_call(kernel, out_shape=shape, compiler_params=PARAMS, **options)(*operands)

    def table_of(count):
        return (2, count * n_dev, block)

    def enter(values):
        kernel = functools.partial(disperse_kernel, rows, total, 0.5, True, load_edge, store_inner)
        shapes = ((n_dev * (halo + 1) * rows * 2, block), table_of(rows))
        matrices = jnp.asarray(np.stack([flat(first[..., edge]), flat(first)]))
        return call_disperse(
            kernel, tuple(jax.ShapeDtypeStruct(shape, f32) for shape in shapes), *(values, matrices, last, betas)
        )

    def go_on(values):
        kernel = functools.partial(disperse_kernel, wide, total, 1.0, False, load_wide, store_wide)
        shape = jax.ShapeDtypeStruct((n_pair * (halo + 1) * wide * 2, block), f32)
        return call_disperse(
            kernel,
            shape,
            *(values, jnp.asarray(flat(first[..., both_halves[0]]))[None], final_wide, last, betas),
            scratch_shapes=[pltpu.VMEM(table_of(wide), f32)],
        )

    def leave(values, turn):
        kernel = functools.partial(disperse_kernel, rows, None, None, True, load_inner, store_edge)
        shape = jax.ShapeDtypeStruct((n_tm, rows, 2, samples), f32)
        matrices = jnp.asarray(np.stack([flat(first), flat(first[:, edge])]))
        return call_disperse(kernel, shape, values, matrices, last, turn)

    def load_spread(ref, h, r, c):
        start = (r // rows) * 2 * (halo + 1) * rows + 2 * (h * rows + r % rows) + c
        return ref[pl.ds(start, n_pair, stride=4 * (halo + 1) * rows), :]

    def load_half(ref, h, r, c):
        return ref[pl.ds(2 * (h * wide + r) + c, n_pair, stride=2 * (halo + 1) * wide), :]

    def store_halves(ref, r, c, values):
        for h in range(2):
            ref[pl.ds(h * n_pair * 2 * wide + 2 * r + c, n_pair, stride=2 * wide), :] = values

    def store_last(ref, r, c, values):
        ref[pl.ds((r // rows) * 2 * rows + 2 * (r % rows) + c, n_pair, stride=4 * rows), :] = values

    def nonlinear(number, windows, profiles):
        is_last = number == ITERS - 1
        height = n_dev * (rows if is_last else wide) * 2
        total_grid, all_modes = modes.shape[1] * n_mode, own_modes * n_mode
        shapes = (
            jax.ShapeDtypeStruct((height, block), f32),
            jax.ShapeDtypeStruct((total_grid, 3 * all_modes), jnp.bfloat16),
            jax.ShapeDtypeStruct((2 * all_modes, total_grid), jnp.bfloat16),
            jax.ShapeDtypeStruct((span, 2 * block), jnp.bfloat16),
        )
        return pl.pallas_call(
            functools.partial(
                nonlinear_kernel,
                wide,
                halo,
                load_half if number else load_spread,
                store_last if is_last else store_halves,
                0 if number else n_mode,
            ),
            out_shape=shapes[0] if number else shapes,
            name="nonlinear",
            compiler_params=PARAMS,
        )(windows, *(profiles if number else (*pieces, jnp.asarray(lags, f32))))

    def exchange(values, groups=None):
        count = len(groups[0]) if groups else n_dev
        shaped = values.reshape(count, -1, 2, block)
        return lax.all_to_all(shaped, BOTH, 0, 0, tiled=True, axis_index_groups=groups).reshape(-1, block)

    entry = field.reshape(own_modes, 2, per_tm, block)
    entry = with_layout_constraint(entry, Layout((0, 2, 1, 3)))
    entry = entry.transpose(0, 2, 1, 3).reshape(n_tm, rows * per_tm, 2, block)
    values = lax.all_to_all(entry, "tm", 0, 0, tiled=True).reshape(-1, block)
    values, half_turn = enter(values)
    values = exchange(values)
    profiles = None
    for number in range(ITERS):
        if number == 0:
            values, *profiles = nonlinear(number, values, None)
        else:
            values = nonlinear(number, values, profiles)
        if number < ITERS - 1:
            values = go_on(exchange(values, both_halves))
            values = exchange(values, halves)
    values = leave(exchange(values), half_turn)
    return lax.all_to_all(values, "tm", 0, 0, tiled=True).reshape(field.shape)


def shards(field, modes, betas):
    n_mode, n_tm = lax.axis_size("mode"), lax.axis_size("tm")
    fits = (
        field.shape[2] % (128 * n_mode) == 0
        and field.shape[0] % n_tm == 0
        and n_tm % 8 == 0
        and modes.shape[1] % 128 == 0
    )
    if not fits:
        return general(field, modes, betas)
    return tiled(field, modes, betas)


def solution(mesh):
    return jax.shard_map(
        shards,
        mesh=mesh,
        in_specs=(P("mode", None, "tm"), P(None, "mode"), P("mode", None)),
        out_specs=P("mode", None, "tm"),
        check_vma=False,
    )
```

```python
import functools
import math

import jax
import jax.numpy as jnp
import numpy as np
from jax import lax
from jax.experimental import pallas as pl
from jax.experimental.layout import Layout, with_layout_constraint
from jax.experimental.pallas import tpu as pltpu
from jax.sharding import PartitionSpec as P


RAMAN_TAPS = 256
ITERS = 2
RAMAN_SHARE = 0.18
KERR_GAIN = 6.0
PRECISE = lax.Precision.HIGHEST
BOTH = ("mode", "tm")
PARAMS = pltpu.CompilerParams(vmem_limit_bytes=16 * 1024 * 1024)


def exp_table(product, length):
    angle = (product % length) * (2.0 * math.pi / length)
    return np.cos(angle), np.sin(angle)


def block_matrix(cosine, sine):
    return np.stack([np.stack([cosine, -sine], 1), np.stack([sine, cosine], 1)], 0)


def raman_taps():
    positions = np.arange(1, RAMAN_TAPS + 1)
    spacing = 256.0 / RAMAN_TAPS
    raw = np.exp(-positions * spacing / 32.0) * np.sin(positions * spacing / 12.2)
    return raw / raw.sum()


def raman_matrix(block, halo):
    taps = raman_taps()
    lag = np.arange(block)[None, :] + halo * block - np.arange((halo + 1) * block)[:, None]
    return np.where((lag >= 1) & (lag <= RAMAN_TAPS), taps[np.clip(lag, 1, RAMAN_TAPS) - 1], 0.0)


def general(field, modes, betas):
    n_mode, n_tm = lax.axis_size("mode"), lax.axis_size("tm")
    t_index = lax.axis_index("tm")
    own_modes, _, samples = field.shape
    n_dev = n_mode * n_tm
    total = samples * n_tm
    block = total // n_dev
    halo = -(-RAMAN_TAPS // block)
    rows = -(-own_modes // n_tm)
    spare = n_tm * rows - own_modes
    f32 = jnp.float32

    dev, pos = np.arange(n_dev), np.arange(block)
    cos_a, sin_a = exp_table(dev[:, None] * dev[None, :], n_dev)
    cos_t, sin_t = exp_table(dev[:, None] * pos[None, :], total)
    cos_b, sin_b = exp_table(pos[:, None] * pos[None, :], block)
    first = jnp.asarray(block_matrix(cos_a, sin_a), f32)
    first_back = jnp.asarray(block_matrix(cos_a, -sin_a) / total, f32)
    last = jnp.asarray(block_matrix(cos_b, sin_b), f32)
    last_back = jnp.asarray(block_matrix(cos_b, -sin_b), f32)
    twist = (jnp.asarray(cos_t, f32), jnp.asarray(sin_t, f32))

    frequency = dev[:, None] + n_dev * pos[None, :]
    norm_freq = jnp.asarray(np.where(frequency < total // 2, frequency, frequency - total) * (2.0 / total), f32)
    rates = lax.dynamic_slice_in_dim(jnp.pad(betas, ((0, spare), (0, 0))), t_index * rows, rows, 0)
    rates = rates[:, :, None, None]
    phase = (
        rates[:, 0]
        + rates[:, 1] * norm_freq
        + rates[:, 2] * (norm_freq * norm_freq) / 2.0
        + rates[:, 3] * (norm_freq * norm_freq * norm_freq) / 6.0
    )
    half_turn = (jnp.cos(phase * 0.5), jnp.sin(phase * 0.5))
    full_turn = (jnp.cos(phase), jnp.sin(phase))

    def disperse(blocks, turn):
        x = jnp.einsum("arcb,cadk->drkb", blocks, first, precision=PRECISE)
        x = jnp.stack([x[0] * twist[0] + x[1] * twist[1], x[1] * twist[0] - x[0] * twist[1]], 0)
        x = jnp.einsum("crkb,cbdq->drkq", x, last, precision=PRECISE)
        x = jnp.stack([x[0] * turn[0] - x[1] * turn[1], x[0] * turn[1] + x[1] * turn[0]], 0)
        x = jnp.einsum("crkq,cqdb->drkb", x, last_back, precision=PRECISE)
        x = jnp.stack([x[0] * twist[0] - x[1] * twist[1], x[1] * twist[0] + x[0] * twist[1]], 0)
        return jnp.einsum("crkb,ckda->ardb", x, first_back, precision=PRECISE)

    raman = jnp.asarray(raman_matrix(block, halo), f32)
    all_profiles = lax.all_gather(modes, "mode", axis=1, tiled=True)
    all_modes = n_mode * own_modes

    def nonlinear(blocks):
        windows = jnp.stack([jnp.roll(blocks, halo - h, axis=0) for h in range(halo + 1)], 3)
        windows = lax.all_to_all(windows, BOTH, 0, 0, tiled=True)
        windows = windows.reshape(n_mode, n_tm * rows, 2, (halo + 1) * block)[:, :own_modes]
        windows = windows.reshape(all_modes, 2, (halo + 1) * block)
        grid = jnp.einsum("pg,pct->cgt", all_profiles, windows, precision=PRECISE)
        intensity = grid[0] * grid[0] + grid[1] * grid[1]
        delayed = jnp.dot(intensity, raman, precision=PRECISE)
        own = slice(halo * block, None)
        weight = (1.0 - RAMAN_SHARE) * intensity[:, own] + RAMAN_SHARE * delayed
        response = jnp.einsum("pg,cgt->pct", all_profiles, grid[:, :, own] * weight, precision=PRECISE)
        values = jnp.stack(
            [
                windows[:, 0, own] - KERR_GAIN * response[:, 1],
                windows[:, 1, own] + KERR_GAIN * response[:, 0],
            ],
            1,
        )
        values = jnp.pad(values.reshape(n_mode, own_modes, 2, block), ((0, 0), (0, spare), (0, 0), (0, 0)))
        return lax.all_to_all(values.reshape(n_dev, rows, 2, block), BOTH, 0, 0, tiled=True)

    entry = jnp.pad(field, ((0, spare), (0, 0), (0, 0))).reshape(n_tm, rows, 2, samples)
    entry = lax.all_to_all(entry, "tm", 0, 0, tiled=True)
    per_tm = samples // block
    blocks = entry.reshape(n_tm, rows, 2, per_tm, block).transpose(0, 3, 1, 2, 4).reshape(n_dev, rows, 2, block)
    blocks = disperse(blocks, half_turn)
    for number in range(ITERS):
        blocks = nonlinear(blocks)
        blocks = disperse(blocks, full_turn if number < ITERS - 1 else half_turn)
    leave = blocks.reshape(n_tm, per_tm, rows, 2, block).transpose(0, 2, 3, 1, 4).reshape(n_tm, rows, 2, samples)
    leave = lax.all_to_all(leave, "tm", 0, 0, tiled=True)
    return leave.reshape(n_tm * rows, 2, samples)[:own_modes]


def split_two(values):
    high = values.astype(jnp.bfloat16)
    return high, (values - high.astype(jnp.float32)).astype(jnp.bfloat16)


def np_split(values):
    high = values.astype(jnp.bfloat16)
    return high, (values - high.astype(np.float64)).astype(jnp.bfloat16)


def product(left, right):
    return jnp.dot(left, right, preferred_element_type=jnp.float32)


def cos_sin(angle):
    quarter = jnp.floor(angle * (2.0 / math.pi) + 0.5)
    rest = angle - quarter * 1.5703125
    rest = rest - quarter * 4.837512969970703e-4
    rest = rest - quarter * 7.549789948768648e-8
    square = rest * rest
    sine = rest + rest * square * (-1.6666654611e-1 + square * (8.3321608736e-3 - square * 1.9515295891e-4))
    cosine = 1.0 - 0.5 * square
    cosine = cosine + square * square * (
        4.166664568298827e-2 + square * (-1.388731625493765e-3 + square * 2.443315711809948e-5)
    )
    turn = quarter.astype(jnp.int32)
    odd = (turn & 1) == 1
    out_cos = jnp.where(odd, sine, cosine)
    out_sin = jnp.where(odd, cosine, sine)
    return (
        jnp.where(((turn + 1) & 2) == 2, -out_cos, out_cos),
        jnp.where((turn & 2) == 2, -out_sin, out_sin),
    )


def work_out_turns(total, share, rows, start, betas_ref, table_ref):
    _, count, block = table_ref.shape
    size = count // rows
    first, last = (lax.broadcasted_iota(jnp.int32, (size, block), d) for d in range(2))
    freq = first + size * last
    freq = jnp.where(freq < total // 2, freq, freq - total).astype(jnp.float32) * (2.0 / total)
    square = freq * freq
    scale = 1.0 / total
    for r in range(rows):
        rates = betas_ref[pl.ds(start + r, 1), :]
        phase = (
            rates[:, 0 : 1]
            + rates[:, 1 : 2] * freq
            + rates[:, 2 : 3] * square / 2.0
            + rates[:, 3 : 4] * (square * freq) / 6.0
        )
        cosine, sine = cos_sin(phase * share)
        part = pl.ds(r * size, size)
        table_ref[0, part] = cosine * scale
        table_ref[1, part] = sine * scale


def make_profiles(rows, pieces, taps_ref, up_ref, down_ref, raman_ref):
    window, double = raman_ref.shape
    block = double // 2
    taps = jnp.broadcast_to(taps_ref[0:1, :], (window, taps_ref.shape[1]))
    taps = pltpu.roll(taps, block, axis=1, stride=1, stride_axis=0)[:, :block]
    raman_ref[...] = jnp.concatenate(split_two(taps), axis=1)
    count = pieces[0].shape[0]
    n_dev = count // rows
    place, mode = (lax.broadcasted_iota(jnp.int32, (count, count), d) for d in range(2))
    order = (mode == (place % n_dev) * rows + place // n_dev).astype(jnp.float32).astype(jnp.bfloat16)
    start = 0
    for piece in pieces:
        width = piece.shape[1]
        wide, low = (product(order, part) for part in split_two(piece[...]))
        down_ref[:, start : start + width] = jnp.concatenate([wide, low], axis=0).astype(jnp.bfloat16)
        stack = jnp.concatenate([wide, low, wide], axis=0)
        up_ref[start : start + width, :] = stack.T.astype(jnp.bfloat16)
        start += width


def disperse_kernel(rows, total, share, joined, load, store, x_ref, *refs):
    count = 1 if joined else 2
    matrices, last_ref, refs = refs[:count], refs[count], refs[count + 1 :]
    n_dev, block = matrices[0].shape[1] // 2, last_ref.shape[0]
    if total is None:
        turn_ref, o_ref = refs
    else:
        betas_ref, o_ref, turn_ref = refs
        place = lax.axis_index("tm")
        holders = betas_ref.shape[0] // rows
        work_out_turns(total, share, rows, place % holders * rows, betas_ref, turn_ref)
        place = place // holders
    cos_high, sin_high, cos_low, sin_low = (last_ref[:, n * block : (n + 1) * block] for n in range(4))
    last_high = jnp.concatenate(
        [jnp.concatenate([cos_high, -sin_high], axis=1), jnp.concatenate([sin_high, cos_high], axis=1)], axis=0
    )
    last_low = jnp.concatenate(
        [jnp.concatenate([cos_low, -sin_low], axis=1), jnp.concatenate([sin_low, cos_low], axis=1)], axis=0
    )
    place_of, time_of = (lax.broadcasted_iota(jnp.int32, (n_dev, block), d) for d in range(2))
    twist = cos_sin((place_of * time_of).astype(jnp.float32) * (2.0 * math.pi / (n_dev * block)))
    twist = [jnp.concatenate([part] * rows, axis=1) for part in twist]

    def across(matrix, values):
        high, low = split_two(values)
        matrix = jnp.concatenate([matrix, matrix[:, : matrix.shape[1] // 2]], axis=1)
        return product(matrix, jnp.concatenate([high, high, low], axis=0))

    def twisted(values):
        re, im = values[:n_dev], values[n_dev:]
        return re * twist[0] + im * twist[1], im * twist[0] - re * twist[1]

    def along(re, im):
        high, low = split_two(jnp.concatenate([re, im], axis=1))
        both = product(jnp.concatenate([high, low], axis=0), last_high)
        size = high.shape[0]
        return both[:size] + both[size:] + product(high, last_low)

    def row_of(values):
        return jnp.concatenate([values[:, r * block : (r + 1) * block] for r in range(rows)], axis=0)

    def lane_of(values):
        return jnp.concatenate([values[r * n_dev : (r + 1) * n_dev] for r in range(rows)], axis=1)

    x = jnp.concatenate(
        [jnp.concatenate([load(x_ref, r, c) for r in range(rows)], axis=1) for c in range(2)], axis=0
    )
    re, im = twisted(across(matrices[0][0], x))
    z = along(row_of(re), row_of(im))
    z_re, z_im = z[:, :block], z[:, block:]
    turn_re, turn_im = turn_ref[0], turn_ref[1]
    z = along(z_re * turn_re - z_im * turn_im, -(z_re * turn_im + z_im * turn_re))
    re, im = twisted(jnp.concatenate([lane_of(z[:, :block]), lane_of(z[:, block:])], axis=0))
    x = across(matrices[0][1] if joined else matrices[1][place], jnp.concatenate([re, im], axis=0))
    for r in range(rows):
        lanes = slice(r * block, (r + 1) * block)
        store(o_ref, r, 0, x[: x.shape[0] // 2, lanes])
        store(o_ref, r, 1, -x[x.shape[0] // 2 :, lanes])


def nonlinear_kernel(rows, halo, load, store, pieces, w_ref, *refs):
    if pieces:
        o_ref, up_ref, down_ref, raman_ref = refs[pieces + 1 :]
        make_profiles(rows, refs[:pieces], refs[pieces], up_ref, down_ref, raman_ref)
    else:
        up_ref, down_ref, raman_ref, o_ref = refs
    block = w_ref.shape[1]
    n_modes = up_ref.shape[1] // 3
    count = n_modes // rows

    def part(h, c):
        return jnp.concatenate([load(w_ref, h, r, c) for r in range(rows)], axis=0)

    own, highs, lows = None, [], []
    for h in range(halo + 1):
        values = jnp.concatenate([part(h, 0), part(h, 1)], axis=1)
        high, low = split_two(values)
        if halo > 1 and h == 0:
            grid = product(up_ref[:, : 2 * n_modes], jnp.concatenate([high, high], axis=0))
        else:
            grid = product(up_ref[...], jnp.concatenate([high, high, low], axis=0))
        g_re, g_im = grid[:, :block], grid[:, block:]
        intensity = g_re * g_re + g_im * g_im
        high, low = split_two(intensity)
        highs.append(high)
        lows.append(low)
        if h == halo:
            own = (values, g_re, g_im, intensity)
    values, g_re, g_im, intensity = own
    taps = raman_ref[...]
    skip = 1 if halo > 1 else 0
    rest = taps[skip * block :, :block]
    taps = jnp.concatenate([taps, jnp.concatenate([rest, jnp.zeros_like(rest)], axis=1)], axis=0)
    both = product(jnp.concatenate(highs + lows[skip:], axis=1), taps)
    weight = (1.0 - RAMAN_SHARE) * intensity + (both[:, :block] + both[:, block:])
    drive = jnp.concatenate([g_re * weight, g_im * weight], axis=1)
    d_high, d_low = split_two(drive)
    both = product(down_ref[...], d_high)
    response = both[:n_modes] + both[n_modes:] + product(down_ref[:n_modes, :], d_low)
    out = [
        values[:, :block] - KERR_GAIN * response[:, block:],
        values[:, block:] + KERR_GAIN * response[:, :block],
    ]
    for c in range(2):
        for r in range(rows):
            store(o_ref, r, c, out[c][r * count : (r + 1) * count])


def tiled(field, modes, betas):
    n_mode, n_tm = lax.axis_size("mode"), lax.axis_size("tm")
    own_modes, _, samples = field.shape
    n_dev = n_mode * n_tm
    total = samples * n_tm
    block = total // n_dev
    halo = -(-RAMAN_TAPS // block)
    rows = own_modes // n_tm
    per_tm = samples // block
    f32 = jnp.float32

    quarter = n_tm // 2
    n_pair = n_mode * quarter
    wide = 2 * rows
    halves = [[m * n_tm + h * quarter + q for m in range(n_mode) for q in range(quarter)] for h in range(2)]
    both_halves = [halves[0] + halves[1]]

    pieces = [modes]
    for shift in range(1, n_mode):
        pieces.append(lax.ppermute(modes, "mode", [(i, (i + shift) % n_mode) for i in range(n_mode)]))
    dev, pos = np.arange(n_dev), np.arange(block)
    cos_a, sin_a = exp_table(dev[:, None] * dev[None, :], n_dev)
    cos_b, sin_b = exp_table(pos[:, None] * pos[None, :], block)
    first = block_matrix(cos_a, sin_a).transpose(2, 3, 0, 1)
    (cos_high, cos_low), (sin_high, sin_low) = np_split(cos_b), np_split(sin_b)
    last = jnp.asarray(np.concatenate([cos_high, sin_high, cos_low, sin_low], axis=1))
    edge = np.arange(n_dev).reshape(n_tm, per_tm).T.reshape(-1)

    def flat(matrix):
        high, low = np_split(matrix.reshape(-1, 2 * n_dev))
        return np.concatenate([high, low], axis=1)

    span = (halo + 1) * block
    lags = np.zeros((8, span + block))
    lags[:, block + 1 : block + 1 + RAMAN_TAPS] = RAMAN_SHARE * raman_taps()

    windows_of = [[(a - halo + h) % n_dev for h in range(halo + 1) for a in devices] for devices in halves]
    final_wide = jnp.asarray(np.stack([flat(first[:, blocks]) for blocks in windows_of]))

    def load_edge(ref, r, c):
        return jnp.concatenate(
            [
                ref[pl.ds(2 * (per_tm * r + q) + c, n_tm, stride=2 * per_tm * rows), :]
                for q in range(per_tm)
            ],
            axis=0,
        )

    def load_inner(ref, r, c):
        return ref[pl.ds(2 * r + c, n_dev, stride=2 * rows), :]

    def store_edge(ref, r, c, values):
        for q in range(per_tm):
            ref[:, r, c, q * block : (q + 1) * block] = values[q * n_tm : (q + 1) * n_tm]

    def store_inner(ref, r, c, values):
        for h in range(halo + 1):
            moved = pltpu.roll(values, halo - h, axis=0) if h < halo else values
            ref[pl.ds(2 * (h * rows + r) + c, n_dev, stride=2 * (halo + 1) * rows), :] = moved

    def load_wide(ref, r, c):
        return ref[pl.ds(2 * r + c, n_dev, stride=2 * wide), :]

    def store_wide(ref, r, c, values):
        for h in range(halo + 1):
            ref[pl.ds(2 * (h * wide + r) + c, n_pair, stride=2 * (halo + 1) * wide), :] = values[
                h * n_pair : (h + 1) * n_pair
            ]

    def call_disperse(kernel, shape, *operands, **options):
        return pl.pallas_call(kernel, out_shape=shape, compiler_params=PARAMS, **options)(*operands)

    def table_of(count):
        return (2, count * n_dev, block)

    def enter(values):
        kernel = functools.partial(disperse_kernel, rows, total, 0.5, True, load_edge, store_inner)
        shapes = ((n_dev * (halo + 1) * rows * 2, block), table_of(rows))
        matrices = jnp.asarray(np.stack([flat(first[..., edge]), flat(first)]))
        return call_disperse(
            kernel, tuple(jax.ShapeDtypeStruct(shape, f32) for shape in shapes), *(values, matrices, last, betas)
        )

    def go_on(values):
        kernel = functools.partial(disperse_kernel, wide, total, 1.0, False, load_wide, store_wide)
        shape = jax.ShapeDtypeStruct((n_pair * (halo + 1) * wide * 2, block), f32)
        return call_disperse(
            kernel,
            shape,
            *(values, jnp.asarray(flat(first[..., both_halves[0]]))[None], final_wide, last, betas),
            scratch_shapes=[pltpu.VMEM(table_of(wide), f32)],
        )

    def leave(values, turn):
        kernel = functools.partial(disperse_kernel, rows, None, None, True, load_inner, store_edge)
        shape = jax.ShapeDtypeStruct((n_tm, rows, 2, samples), f32)
        matrices = jnp.asarray(np.stack([flat(first), flat(first[:, edge])]))
        return call_disperse(kernel, shape, values, matrices, last, turn)

    def load_spread(ref, h, r, c):
        start = (r // rows) * 2 * (halo + 1) * rows + 2 * (h * rows + r % rows) + c
        return ref[pl.ds(start, n_pair, stride=4 * (halo + 1) * rows), :]

    def load_half(ref, h, r, c):
        return ref[pl.ds(2 * (h * wide + r) + c, n_pair, stride=2 * (halo + 1) * wide), :]

    def store_halves(ref, r, c, values):
        for h in range(2):
            ref[pl.ds(h * n_pair * 2 * wide + 2 * r + c, n_pair, stride=2 * wide), :] = values

    def store_last(ref, r, c, values):
        ref[pl.ds((r // rows) * 2 * rows + 2 * (r % rows) + c, n_pair, stride=4 * rows), :] = values

    def nonlinear(number, windows, profiles):
        is_last = number == ITERS - 1
        height = n_dev * (rows if is_last else wide) * 2
        total_grid, all_modes = modes.shape[1] * n_mode, own_modes * n_mode
        shapes = (
            jax.ShapeDtypeStruct((height, block), f32),
            jax.ShapeDtypeStruct((total_grid, 3 * all_modes), jnp.bfloat16),
            jax.ShapeDtypeStruct((2 * all_modes, total_grid), jnp.bfloat16),
            jax.ShapeDtypeStruct((span, 2 * block), jnp.bfloat16),
        )
        return pl.pallas_call(
            functools.partial(
                nonlinear_kernel,
                wide,
                halo,
                load_half if number else load_spread,
                store_last if is_last else store_halves,
                0 if number else n_mode,
            ),
            out_shape=shapes[0] if number else shapes,
            name="nonlinear",
            compiler_params=PARAMS,
        )(windows, *(profiles if number else (*pieces, jnp.asarray(lags, f32))))

    def exchange(values, groups=None):
        count = len(groups[0]) if groups else n_dev
        shaped = values.reshape(count, -1, 2, block)
        return lax.all_to_all(shaped, BOTH, 0, 0, tiled=True, axis_index_groups=groups).reshape(-1, block)

    entry = field.reshape(own_modes, 2, per_tm, block)
    entry = with_layout_constraint(entry, Layout((0, 2, 1, 3)))
    entry = entry.transpose(0, 2, 1, 3).reshape(n_tm, rows * per_tm, 2, block)
    values = lax.all_to_all(entry, "tm", 0, 0, tiled=True).reshape(-1, block)
    values, half_turn = enter(values)
    values = exchange(values)
    profiles = None
    for number in range(ITERS):
        if number == 0:
            values, *profiles = nonlinear(number, values, None)
        else:
            values = nonlinear(number, values, profiles)
        if number < ITERS - 1:
            values = go_on(exchange(values, both_halves))
            values = exchange(values, halves)
    values = leave(exchange(values), half_turn)
    return lax.all_to_all(values, "tm", 0, 0, tiled=True).reshape(field.shape)


def shards(field, modes, betas):
    n_mode, n_tm = lax.axis_size("mode"), lax.axis_size("tm")
    fits = (
        field.shape[2] % (128 * n_mode) == 0
        and field.shape[0] % n_tm == 0
        and n_tm % 8 == 0
        and modes.shape[1] % 128 == 0
    )
    if not fits:
        return general(field, modes, betas)
    return tiled(field, modes, betas)


def solution(mesh):
    return jax.shard_map(
        shards,
        mesh=mesh,
        in_specs=(P("mode", None, "tm"), P(None, "mode"), P("mode", None)),
        out_specs=P("mode", None, "tm"),
        check_vma=False,
    )
```
